32 devices in a mesh: rows: 8 (over z, x), grp: 4 (over y, core).
Axes of the slice: x: 2, y: 2, z: 4, core: 2. Of those that a mesh axis runs over, the one named last changes fastest.
Arguments:
- vectors: bfloat16 [64, 131072], P(None, 'rows'), may hold values from -6 to 6
- wear_freq: bfloat16 [131072], P('rows'), may hold values from 0 to 400
- param_scale: bfloat16 [131072], P('rows'), may hold values from 0.29882812 to 3
- row_angle: bfloat16 [32768], P(('rows', 'grp')), may hold values from -3.140625 to 3.140625
- row_weight: bfloat16 [32768], P(('rows', 'grp')), may hold values from 0.29882812 to 3
- entry_block: int32 [4096], P(('rows', 'grp')), may hold values from 0 to 255, as said below
- entry_row: int32 [4096], P(('rows', 'grp')), may hold values from 0 to 3
- entry_count: int32 [32], P(('rows', 'grp')), may hold values from 16 to 128, as said below
- block_home: int32 [256], replicated, may hold values from 0 to 255, as said below
Outputs:
- product: float32 [64, 131072], P(None, 'rows')
The draws below stay inside these ranges and needn't reach their ends.
Inputs may be any that keep to these rules, and one draw needn't show every extreme that they name: block_home is a permutation of the 256 parameter blocks. Among the live entries of one group at most 16 have block_home[entry_block] // 32 equal to any one value; a group with 128 live entries reaches 16 for every value. `entry_count`: in every draw some group has 128 live entries.
All inputs are finite; a program needn't handle non-finite values.
Results may differ from the reference program's by a relative error of at most 0.0036.
Values may be sent and summed in bfloat16 or wider, within the bound.
No kernel may reach another device: no remote copies, remote signals or barrier semaphores. Data moves between devices by JAX's collectives and lax.ppermute only.
A program may use at most 128 MiB of HBM per device.

```python
import math
import jax
import jax.numpy as jnp
from jax import lax

KRY = 64
BLK_R = 256
BLK_P = 512
PB_DEV = 32
RB_DEV = 4
SLOTS = 128
GROUPS = 32
NPB = 256
PARAMS = 131072
RESID = 32768
N_ROWS = 8
N_GRP = 4


def shared_home(key):
    return jax.random.permutation(jax.random.fold_in(key, 11), NPB).astype(jnp.int32)


def draw_block_home(key, part):
    return shared_home(key)


def one_order(subkey):
    return jax.random.permutation(subkey, SLOTS).astype(jnp.int32)


def draw_entry_block(key, part):
    home = shared_home(key)
    inverse = jnp.zeros((NPB,), jnp.int32).at[home].set(jnp.arange(NPB, dtype=jnp.int32))
    groups = N_ROWS * N_GRP
    subkeys = jax.random.split(jax.random.fold_in(key, 12), groups)
    orders = jax.vmap(one_order)(subkeys)
    owners = orders % N_ROWS
    local_pick = jax.random.randint(jax.random.fold_in(key, 13), (groups, SLOTS), 0, PB_DEV).astype(jnp.int32)
    stored = owners * PB_DEV + local_pick
    return inverse[stored].reshape(groups * SLOTS)


def draw_entry_count(key, part):
    groups = N_ROWS * N_GRP
    lowest = SLOTS // 8
    first = jax.random.randint(jax.random.fold_in(key, 21), (groups,), 0, SLOTS - lowest + 1)
    second = jax.random.randint(jax.random.fold_in(key, 22), (groups,), 0, SLOTS - lowest + 1)
    counts = lowest + jnp.minimum(first, second)
    fullest = jax.random.randint(jax.random.fold_in(key, 23), (), 0, groups)
    counts = jnp.where(jnp.arange(groups) == fullest, SLOTS, counts)
    return counts.astype(jnp.int32)


def plant(entries, own_key, low, high):
    spot = [jax.random.randint(jax.random.fold_in(own_key, axis), (), 0, length) for axis, length in enumerate(entries.shape)]
    main_axis = entries.shape.index(max(entries.shape))
    neighbour = spot[:main_axis] + [(spot[main_axis] + 1) % entries.shape[main_axis]] + spot[main_axis + 1:]
    return entries.at[tuple(spot)].set(low).at[tuple(neighbour)].set(high)


def block_levels(rng, shape, pieces, smallest, largest):
    def one(axis_at, parts):
        heights = jax.random.uniform(jax.random.fold_in(jax.random.fold_in(rng, 6), axis_at), (parts,), jnp.float32, smallest / len(pieces), largest / len(pieces))
        return jnp.repeat(jnp.exp(heights), shape[axis_at] // parts).reshape((-1,) + (1,) * (len(shape) - axis_at - 1))

    factor_of = one(*pieces[0])
    for cut in pieces[1:]:
        factor_of = factor_of * one(*cut)
    return factor_of


def scatter_about(key, shape, scale, bound, pieces=(), kind=jnp.bfloat16):
    loudness = block_levels(key, shape, pieces, -0.22, 0.18) if pieces else 1.0
    array = jax.random.normal(key, shape, jnp.float32) * scale * loudness
    return jnp.minimum(jnp.maximum(array, -bound), bound).astype(kind)


def setup_inputs(seed: int = 0) -> dict:
    streams_of = jax.random.split(jax.random.key(seed), 10)
    vectors = scatter_about(streams_of[0], (KRY, PARAMS), 1.0, 6.0, ((1, 8),))
    wear_freq = jnp.clip(400.0 * jax.random.uniform(streams_of[1], (PARAMS,), jnp.float32) ** block_levels(streams_of[1], (PARAMS,), ((0, 8),), -0.2, 0.2), 0.0, 400.0).astype(jnp.bfloat16)
    param_scale = jnp.clip(jnp.exp(math.log(3.0) - 2.306499 * jax.random.uniform(streams_of[2], (PARAMS,), jnp.float32) ** block_levels(streams_of[2], (PARAMS,), ((0, 8),), -0.2, 0.2)), 0.29882812, 3.0).astype(jnp.bfloat16)
    row_angle = jnp.clip(jax.random.uniform(streams_of[3], (RESID,), jnp.float32, -3.140625, 3.140625), -3.140625, 3.140625).astype(jnp.bfloat16)
    row_weight = jnp.clip(jnp.exp(math.log(3.0) - 2.306499 * jax.random.uniform(streams_of[4], (RESID,), jnp.float32) ** block_levels(streams_of[4], (RESID,), ((0, 32),), -0.2, 0.2)), 0.29882812, 3.0).astype(jnp.bfloat16)
    entry_block = draw_entry_block(jax.random.fold_in(streams_of[9], 71), 0)
    entry_row = plant(jax.random.randint(streams_of[6], (GROUPS * SLOTS,), 0, RB_DEV), jax.random.fold_in(streams_of[6], 1), 0, RB_DEV - 1).astype(jnp.int32)
    entry_count = draw_entry_count(jax.random.fold_in(streams_of[9], 71), 0)
    block_home = draw_block_home(jax.random.fold_in(streams_of[9], 71), 0)
    return dict(vectors=vectors, wear_freq=wear_freq, param_scale=param_scale, row_angle=row_angle, row_weight=row_weight, entry_block=entry_block, entry_row=entry_row, entry_count=entry_count, block_home=block_home)


def jacobian(angles, weights, harmonics, scales):
    phase = angles.astype(jnp.float32)[..., :, None] * harmonics.astype(jnp.float32)[..., None, :]
    factor = 1.0 / math.sqrt(8.0 * BLK_P)
    values = weights.astype(jnp.float32)[..., :, None] * scales.astype(jnp.float32)[..., None, :] * jnp.cos(phase) * factor
    return values.astype(jnp.bfloat16)

def reference(vectors, wear_freq, param_scale, row_angle, row_weight, entry_block, entry_row, entry_count, block_home):
    blocks_all = block_home.shape[0]
    groups = entry_count.shape[0]
    vector_blocks = vectors.reshape(KRY, blocks_all, BLK_P)
    harmonic_blocks = wear_freq.reshape(blocks_all, BLK_P)
    scale_blocks = param_scale.reshape(blocks_all, BLK_P)
    angle_rows = row_angle.reshape(groups, RB_DEV, BLK_R)
    weight_rows = row_weight.reshape(groups, RB_DEV, BLK_R)
    block_ids = entry_block.reshape(groups, SLOTS)
    row_ids = entry_row.reshape(groups, SLOTS)
    slot_ids = jnp.arange(SLOTS, dtype=jnp.int32)
    row_range = jnp.arange(RB_DEV, dtype=jnp.int32)

    def one_group(total, inputs):
        angles, weights, blocks, row_pick, count = inputs
        stored = block_home[blocks].astype(jnp.int32)
        live = slot_ids < count
        jac = jacobian(angles[row_pick], weights[row_pick], harmonic_blocks[stored], scale_blocks[stored]).astype(jnp.float32)
        chosen = jnp.transpose(vector_blocks[:, stored, :], (1, 0, 2)).astype(jnp.float32)
        terms = jnp.einsum('skp,srp->skr', chosen, jac)
        terms = jnp.where(live[:, None, None], terms, 0.0)
        member = ((row_pick[:, None] == row_range[None, :]) & live[:, None]).astype(jnp.float32)
        outputs = jnp.einsum('sb,skr->bkr', member, terms, precision=lax.Precision.HIGHEST).astype(jnp.bfloat16)
        back = jnp.einsum('skr,srp->skp', outputs[row_pick].astype(jnp.float32), jac)
        back = jnp.where(live[:, None, None], back, 0.0)
        return (total.at[stored].add(back), None)
    start = jnp.zeros((blocks_all, KRY, BLK_P), jnp.float32)
    total, unused = lax.scan(one_group, start, (angle_rows, weight_rows, block_ids, row_ids, entry_count))
    return jnp.transpose(total, (1, 0, 2)).reshape(KRY, blocks_all * BLK_P)
```

```python
import functools
import math

import jax
import jax.numpy as jnp
from jax import lax
from jax.experimental import pallas as pl
from jax.experimental.pallas import tpu as pltpu
from jax.sharding import PartitionSpec as P

BLK_R = 256
BLK_P = 512
PIECES = 8
RING = 8
VMEM_LIMIT = 40 << 20

f32 = jnp.float32
bf16 = jnp.bfloat16

COS_POLY = (
    1.4142134965678816,
    -6.978850988354285,
    5.7394611717976565,
    -1.8835629903409246,
    0.3106981920279389,
)
ROUNDER = 12582912.0


def turn_constants():
    constants = []
    rest = 1.0 / (2.0 * math.pi)
    for _ in range(3):
        mantissa, exponent = math.frexp(rest)
        constant = math.ldexp(round(mantissa * 256.0) / 256.0, exponent)
        constants.append(constant)
        rest -= constant
    return constants


def angle_pieces(angles):
    out = []
    for constant in turn_constants():
        exact = angles * constant
        top = lax.reduce_precision(exact, 8, 7)
        out += [top, exact - top]
    return out


def collect(codes, todo, wanted=None):
    def visit(place, found):
        todo[found] = place
        code = codes[place]
        take = code >= 0
        if wanted is not None:
            take = take & wanted(code)
        return found + take.astype(jnp.int32)

    return lax.fori_loop(0, codes.shape[0], visit, 0)


def forward_kernel(
    blocks, capacity, codes, left, right, turned, part, jac, todo, even, odd, sems
):
    spare = codes.shape[0]
    part[...] = jnp.zeros_like(part)
    found = collect(codes, todo)
    steps = (found + 1) // 2

    def decode(place):
        code = codes[place]
        return lax.rem(code, blocks), lax.div(code, blocks), lax.div(place, capacity)

    def make(buffer, place):
        block, row, group = decode(place)
        angles = left[group, :, pl.ds(pl.multiple_of(row * BLK_R, BLK_R), BLK_R)]
        both = lax.dot_general(
            angles, right[block], (((0,), (0,)), ((), ())), preferred_element_type=f32
        )
        turns, weight = both[:, :BLK_P], both[:, BLK_P:]
        rest = turns - ((turns + ROUNDER) - ROUNDER)
        square = rest * rest
        root = COS_POLY[4] * square + COS_POLY[3]
        for k in (2, 1, 0):
            root = root * square + COS_POLY[k]
        buffer[...] = (weight * (root * root - 1.0)).astype(bf16)

    def apply(buffer, place, keep):
        block, row, group = decode(place)
        chosen = turned[pl.ds(pl.multiple_of(block * BLK_P, BLK_P), BLK_P), :]
        term = jnp.dot(buffer[...], chosen, preferred_element_type=f32)
        if keep is not None:
            term = jnp.where(keep, term, 0.0)
        part[group, :, pl.ds(pl.multiple_of(row * BLK_R, BLK_R), BLK_R)] += term.T

    def save(buffer, parity, which, place):
        return pltpu.make_async_copy(buffer.at[parity], jac.at[place], sems.at[parity, which])

    def step(turn, before):
        parity = lax.rem(turn, 2)
        first = todo[2 * turn]
        paired = 2 * turn + 1 < found
        second = todo[jnp.where(paired, 2 * turn + 1, 2 * turn)]

        @pl.when(turn >= 2)
        def _():
            save(even, parity, 0, 0).wait()
            save(odd, parity, 1, 0).wait()

        apply(odd.at[1 - parity], before, turn > 0)
        make(even.at[parity], first)
        save(even, parity, 0, first).start()
        apply(even.at[parity], first, None)
        make(odd.at[parity], second)
        save(odd, parity, 1, jnp.where(paired, second, spare)).start()
        return second

    last = lax.fori_loop(0, steps, step, 0)

    @pl.when((found > 0) & (lax.rem(found, 2) == 0))
    def _():
        apply(odd.at[lax.rem(steps + 1, 2)], last, None)

    for back in (1, 2):
        @pl.when(steps >= back)
        def _():
            parity = lax.rem(steps + back, 2)
            save(even, parity, 0, 0).wait()
            save(odd, parity, 1, 0).wait()


def forward(codes, left, right, turned, capacity):
    groups, _, width = left.shape
    blocks = right.shape[0]
    room = codes.shape[0]
    vector_count = turned.shape[1]
    vmem = pl.BlockSpec(memory_space=pltpu.VMEM)
    return pl.pallas_call(
        functools.partial(forward_kernel, blocks, capacity),
        out_shape=(
            jax.ShapeDtypeStruct((groups, vector_count, width), f32),
            jax.ShapeDtypeStruct((room + 1, BLK_R, BLK_P), bf16),
        ),
        in_specs=[pl.BlockSpec(memory_space=pltpu.SMEM), vmem, vmem, vmem],
        out_specs=(vmem, pl.BlockSpec(memory_space=pl.ANY)),
        scratch_shapes=[
            pltpu.SMEM((room + 1,), jnp.int32),
            pltpu.VMEM((2, BLK_R, BLK_P), bf16),
            pltpu.VMEM((2, BLK_R, BLK_P), bf16),
            pltpu.SemaphoreType.DMA((2, 2)),
        ],
        compiler_params=pltpu.CompilerParams(vmem_limit_bytes=VMEM_LIMIT),
        name="forward",
    )(codes, left, right, turned)


def backward_kernel(blocks, capacity, codes, half, gathered, jac, out, todo, ring, sems):
    per_half = blocks // 2
    depth = ring.shape[0]
    found = collect(codes, todo, lambda code: lax.div(lax.rem(code, blocks), per_half) == half[0])

    def load(turn):
        slot = lax.rem(turn, depth)
        return pltpu.make_async_copy(jac.at[todo[turn]], ring.at[slot], sems.at[slot])

    def prime(turn, carry):
        load(turn).start()
        return carry

    lax.fori_loop(0, jnp.minimum(found, depth - 1), prime, 0)
    out[...] = jnp.zeros_like(out)

    def step(turn, carry):
        @pl.when(turn + depth - 1 < found)
        def _():
            load(turn + depth - 1).start()

        place = todo[turn]
        code = codes[place]
        block, row = lax.rem(lax.rem(code, blocks), per_half), lax.div(code, blocks)
        group = lax.div(place, capacity)
        chosen = gathered[group, :, pl.ds(pl.multiple_of(row * BLK_R, BLK_R), BLK_R)]
        at = pl.ds(pl.multiple_of(block * BLK_P, BLK_P), BLK_P)
        load(turn).wait()
        out[:, at] += jnp.dot(chosen, ring[lax.rem(turn, depth)], preferred_element_type=f32)
        return carry

    lax.fori_loop(0, found, step, 0)


def backward(codes, half, gathered, jac, blocks, capacity):
    smem = pl.BlockSpec(memory_space=pltpu.SMEM)
    vmem = pl.BlockSpec(memory_space=pltpu.VMEM)
    return pl.pallas_call(
        functools.partial(backward_kernel, blocks, capacity),
        out_shape=jax.ShapeDtypeStruct((gathered.shape[1], blocks // 2 * BLK_P), f32),
        in_specs=[smem, smem, vmem, pl.BlockSpec(memory_space=pl.ANY)],
        out_specs=vmem,
        scratch_shapes=[
            pltpu.SMEM((codes.shape[0] + 1,), jnp.int32),
            pltpu.VMEM((RING, BLK_R, BLK_P), bf16),
            pltpu.SemaphoreType.DMA((RING,)),
        ],
        compiler_params=pltpu.CompilerParams(vmem_limit_bytes=VMEM_LIMIT),
        name="backward",
    )(codes, half, gathered, jac)


def swap(array, axis, bit):
    return lax.ppermute(array, axis, [(i, i ^ bit) for i in range(lax.axis_size(axis))])


def body(
    vectors,
    wear_freq,
    param_scale,
    row_angle,
    row_weight,
    entry_block,
    entry_row,
    entry_count,
    block_home,
):
    holders = lax.axis_size("rows")
    members = lax.axis_size("grp")
    vector_count = vectors.shape[0]
    blocks_here = vectors.shape[1] // BLK_P
    slots = entry_block.shape[0]
    capacity = slots // holders
    width = row_angle.shape[0]

    names = jnp.arange(block_home.shape[0], dtype=jnp.int32)
    stored = jnp.sum(
        jnp.where(entry_block[:, None] == names[None, :], block_home[None, :], 0), axis=1
    )
    slot_ids = jnp.arange(slots, dtype=jnp.int32)
    live = slot_ids < entry_count[0]
    holder = jnp.where(live, stored // blocks_here, -1)
    earlier = (holder[:, None] == holder[None, :]) & (slot_ids[None, :] < slot_ids[:, None])
    places = jnp.sum(earlier.astype(jnp.int32), axis=1)
    code = entry_row * blocks_here + stored % blocks_here
    target = jnp.where(live, holder * capacity + places, -1)
    room_ids = jnp.arange(holders * capacity, dtype=jnp.int32)
    wanted = (
        jnp.sum(jnp.where(target[None, :] == room_ids[:, None], code[None, :] + 1, 0), axis=1) - 1
    )
    wanted = wanted.reshape(holders, 1, capacity).astype(f32)

    angle_rows = jnp.stack(
        angle_pieces(row_angle.astype(f32)) + [row_weight.astype(f32)], axis=0
    )
    send = jnp.concatenate(
        [
            jnp.broadcast_to(angle_rows[None], (holders, PIECES - 1, width)),
            jnp.pad(wanted, ((0, 0), (0, 0), (0, width - capacity))),
        ],
        axis=1,
    ).astype(bf16)
    left = lax.all_to_all(send, "rows", split_axis=0, concat_axis=0, tiled=True)
    codes = left[:, PIECES - 1, :capacity].astype(jnp.int32).reshape(holders * capacity)

    freq = wear_freq.reshape(blocks_here, 1, BLK_P)
    scale = (param_scale.astype(f32) * (1.0 / math.sqrt(8.0 * BLK_P))).astype(bf16)
    scale = scale.reshape(blocks_here, 1, BLK_P)
    kind = lax.broadcasted_iota(jnp.int32, (1, PIECES, 1), 1)
    right = jnp.concatenate(
        [
            jnp.where(kind < PIECES - 2, freq, jnp.zeros_like(freq)),
            jnp.where(kind == PIECES - 2, scale, jnp.zeros_like(scale)),
        ],
        axis=2,
    )
    part, jac = forward(codes, left, right, vectors.T, capacity)

    pieces = lax.all_to_all(part, "rows", split_axis=0, concat_axis=0, tiled=True)
    outputs = jnp.sum(pieces, axis=0).astype(bf16)
    gathered = lax.all_gather(outputs, "rows")

    core = lax.axis_index("grp") % 2
    give = backward(codes, (1 - core).reshape(1), gathered, jac, blocks_here, capacity)
    got = swap(give, "grp", 1)
    keep = backward(codes, core.reshape(1), gathered, jac, blocks_here, capacity)
    half_sum = keep + got
    bit = 2
    while bit < members:
        rounded = lax.reduce_precision(half_sum, 8, 7)
        half_sum = rounded + swap(rounded.astype(bf16), "grp", bit).astype(f32)
        bit *= 2
    other = swap(half_sum, "grp", 1)
    first = core == 0
    return jnp.concatenate(
        [jnp.where(first, half_sum, other), jnp.where(first, other, half_sum)], axis=1
    )


def solution(mesh):
    return jax.shard_map(
        body,
        mesh=mesh,
        in_specs=(
            P(None, "rows"),
            P("rows"),
            P("rows"),
            P(("rows", "grp")),
            P(("rows", "grp")),
            P(("rows", "grp")),
            P(("rows", "grp")),
            P(("rows", "grp")),
            P(),
        ),
        out_specs=P(None, "rows"),
        check_vma=False,
    )
```

```python
import functools
import math

import jax
import jax.numpy as jnp
from jax import lax
from jax.experimental import pallas as pl
from jax.experimental.pallas import tpu as pltpu
from jax.sharding import PartitionSpec as P

BLK_R = 256
BLK_P = 512
PIECES = 8
RING = 8
VMEM_BASE = 12 << 20

f32 = jnp.float32
bf16 = jnp.bfloat16

COS_POLY = (
    1.4142134965678816,
    -6.978850988354285,
    5.7394611717976565,
    -1.8835629903409246,
    0.3106981920279389,
)
ROUNDER = 12582912.0


def turn_constants():
    constants = []
    rest = 1.0 / (2.0 * math.pi)
    for _ in range(3):
        mantissa, exponent = math.frexp(rest)
        constant = math.ldexp(round(mantissa * 256.0) / 256.0, exponent)
        constants.append(constant)
        rest -= constant
    return constants


def angle_pieces(angles):
    out = []
    for constant in turn_constants():
        exact = angles * constant
        top = lax.reduce_precision(exact, 8, 7)
        out += [top, exact - top]
    return out


def collect(codes, todo, wanted):
    def visit(place, found):
        todo[found] = place
        code = codes[place]
        return found + ((code >= 0) & wanted(place, code)).astype(jnp.int32)

    return lax.fori_loop(0, codes.shape[0], visit, 0)


def entry_cost(entries, vector_count):
    return pl.CostEstimate(flops=entries, bytes_accessed=vector_count, transcendentals=0)


def forward_kernel(
    blocks,
    capacity,
    ring,
    splits,
    codes,
    where,
    left,
    right,
    vectors,
    *refs,
):
    *parts, jac, todo, part, even, odd, sems = refs
    spare = codes.shape[0]
    part[...] = jnp.zeros_like(part)

    def wanted(place, code):
        return lax.rem(lax.div(place, capacity), 2) == where[1]

    found = collect(codes, todo, wanted)
    steps = (found + 1) // 2

    def decode(place):
        code = codes[place]
        position = lax.div(place, 2 * capacity)
        behind = lax.rem(where[0] - 1 - position + 2 * ring, ring)
        return lax.rem(code, blocks), lax.div(code, blocks), lax.div(place, capacity), behind

    def make(buffer, place):
        block, row, group, _ = decode(place)
        angles = left[group, :, pl.ds(pl.multiple_of(row * BLK_R, BLK_R), BLK_R)]
        both = lax.dot_general(
            angles, right[block], (((0,), (0,)), ((), ())), preferred_element_type=f32
        )
        turns, weight = both[:, :BLK_P], both[:, BLK_P:]
        rest = turns - ((turns + ROUNDER) - ROUNDER)
        square = rest * rest
        root = COS_POLY[4] * square + COS_POLY[3]
        for k in (2, 1, 0):
            root = root * square + COS_POLY[k]
        buffer[...] = (weight * (root * root - 1.0)).astype(bf16)

    def apply(buffer, place, keep):
        block, row, _, behind = decode(place)
        chosen = vectors[:, pl.ds(pl.multiple_of(block * BLK_P, BLK_P), BLK_P)]
        term = lax.dot_general(
            buffer[...], chosen, (((1,), (1,)), ((), ())), preferred_element_type=f32
        )
        if keep is not None:
            term = jnp.where(keep, term, 0.0)
        part[behind, :, pl.ds(pl.multiple_of(row * BLK_R, BLK_R), BLK_R)] += term.T

    def save(buffer, parity, which, place):
        return pltpu.make_async_copy(buffer.at[parity], jac.at[place], sems.at[parity, which])

    def step(turn, before):
        parity = lax.rem(turn, 2)
        first = todo[2 * turn]
        paired = 2 * turn + 1 < found
        second = todo[jnp.where(paired, 2 * turn + 1, 2 * turn)]

        @pl.when(turn >= 2)
        def _():
            save(even, parity, 0, 0).wait()
            save(odd, parity, 1, 0).wait()

        apply(odd.at[1 - parity], before, turn > 0)
        make(even.at[parity], first)
        save(even, parity, 0, first).start()
        apply(even.at[parity], first, None)
        make(odd.at[parity], second)
        save(odd, parity, 1, jnp.where(paired, second, spare)).start()
        return second

    last = lax.fori_loop(0, steps, step, 0)

    @pl.when((found > 0) & (lax.rem(found, 2) == 0))
    def _():
        apply(odd.at[lax.rem(steps + 1, 2)], last, None)

    for back in (1, 2):
        @pl.when(steps >= back)
        def _():
            parity = lax.rem(steps + back, 2)
            save(even, parity, 0, 0).wait()
            save(odd, parity, 1, 0).wait()

    each = ring // splits
    for k in range(splits):
        parts[k][...] = part[k * each : (k + 1) * each]


def forward(codes, where, left, right, vectors, capacity, splits):
    groups, _, width = left.shape
    ring = groups // 2
    blocks = right.shape[0]
    room = codes.shape[0]
    count = vectors.shape[0]
    vmem = pl.BlockSpec(memory_space=pltpu.VMEM)
    smem = pl.BlockSpec(memory_space=pltpu.SMEM)
    return pl.pallas_call(
        functools.partial(forward_kernel, blocks, capacity, ring, splits),
        out_shape=(jax.ShapeDtypeStruct((ring // splits, count, width), f32),) * splits
        + (pltpu.HBM((room + 1, BLK_R, BLK_P), bf16),),
        in_specs=[smem, smem, vmem, vmem, vmem],
        out_specs=(vmem,) * splits + (pl.BlockSpec(memory_space=pltpu.HBM),),
        scratch_shapes=[
            pltpu.SMEM((room + 1,), jnp.int32),
            pltpu.VMEM((ring, count, width), f32),
            pltpu.VMEM((2, BLK_R, BLK_P), bf16),
            pltpu.VMEM((2, BLK_R, BLK_P), bf16),
            pltpu.SemaphoreType.DMA((2, 2)),
        ],
        compiler_params=pltpu.CompilerParams(
            vmem_limit_bytes=VMEM_BASE + 12 * ring * count * width
        ),
        cost_estimate=entry_cost(room // 4, count),
        name="forward",
    )(codes, where, left, right, vectors)


def backward_kernel(blocks, capacity, ring, codes, where, near_jac, far_jac, *refs):
    *pieces, out, gathered, todo, buffers, sems = refs
    here = out.shape[1] // BLK_P
    depth = buffers.shape[0]

    def wanted(place, code):
        block = lax.rem(code, blocks)
        return (block >= where[2]) & (block < where[2] + here)

    found = collect(codes, todo, wanted)

    def is_near(place):
        return lax.rem(lax.div(place, capacity), 2) == where[1]

    def start(turn):
        slot = lax.rem(turn, depth)
        place = todo[turn]

        @pl.when(is_near(place))
        def _():
            pltpu.make_async_copy(near_jac.at[place], buffers.at[slot], sems.at[slot]).start()

        @pl.when(~is_near(place))
        def _():
            pltpu.make_async_copy(far_jac.at[place], buffers.at[slot], sems.at[slot]).start()

    def prime(turn, carry):
        start(turn)
        return carry

    lax.fori_loop(0, jnp.minimum(found, depth - 1), prime, 0)
    for k in range(len(pieces)):
        gathered[k] = pieces[k][...]
    out[...] = jnp.zeros_like(out)

    def step(turn, carry):
        @pl.when(turn + depth - 1 < found)
        def _():
            start(turn + depth - 1)

        place = todo[turn]
        code = codes[place]
        block, row = lax.rem(code, blocks) - where[2], lax.div(code, blocks)
        behind = lax.rem(where[0] - lax.div(place, 2 * capacity) + ring, ring)
        piece = jnp.where(is_near(place), behind, ring + behind)
        chosen = gathered[piece, :, pl.ds(pl.multiple_of(row * BLK_R, BLK_R), BLK_R)]
        at = pl.ds(pl.multiple_of(block * BLK_P, BLK_P), BLK_P)
        slot = lax.rem(turn, depth)
        pltpu.make_async_copy(near_jac.at[0], buffers.at[slot], sems.at[slot]).wait()
        out[:, at] += jnp.dot(chosen, buffers[slot], preferred_element_type=f32)
        return carry

    lax.fori_loop(0, found, step, 0)


def joined_backward_kernel(blocks, capacity, ring, *refs):
    *inputs, gathered, out, todo, buffers, sems = refs
    backward_kernel(blocks, capacity, ring, *inputs, out, gathered, todo, buffers, sems)


def backward(codes, where, near_jac, far_jac, pieces, blocks, here, capacity):
    joined = not isinstance(pieces, list)
    smem = pl.BlockSpec(memory_space=pltpu.SMEM)
    vmem = pl.BlockSpec(memory_space=pltpu.VMEM)
    hbm = pl.BlockSpec(memory_space=pl.ANY)
    sources = [pieces] if joined else pieces
    count, width = sources[0].shape[-2:]
    total = pieces.shape[0] if joined else len(pieces)
    terms = jax.ShapeDtypeStruct((count, here * BLK_P), f32)
    gathered = jax.ShapeDtypeStruct((total, count, width), bf16)
    kernel = joined_backward_kernel if joined else backward_kernel
    result = pl.pallas_call(
        functools.partial(kernel, blocks, capacity, total // 2),
        out_shape=terms if joined else (terms, gathered),
        in_specs=[smem, smem, hbm, hbm] + [vmem] * len(sources),
        out_specs=vmem if joined else (vmem, vmem),
        scratch_shapes=[
            pltpu.SMEM((codes.shape[0] + 1,), jnp.int32),
            pltpu.VMEM((RING, BLK_R, BLK_P), bf16),
            pltpu.SemaphoreType.DMA((RING,)),
        ],
        compiler_params=pltpu.CompilerParams(vmem_limit_bytes=36 << 20),
        cost_estimate=entry_cost(codes.shape[0] // 8, count),
        name="backward",
    )(codes, where, near_jac, far_jac, *sources)
    return (result, pieces) if joined else result


def place_kernel(quarters, where, *refs):
    *sources, out, sems = refs
    sources = sources[-len(quarters) :]
    wide = sources[0].shape[1]
    copies = []
    for k, (mine, chunk) in enumerate(quarters):
        half = where[0] if mine else 1 - where[0]
        at = pl.ds(pl.multiple_of((2 * half + chunk) * wide, wide), wide)
        copies.append(pltpu.make_async_copy(sources[k], out.at[:, at], sems.at[k]))
    for copy in copies:
        copy.start()
    for copy in copies:
        copy.wait()


def place(where, into, quarters, sources):
    hbm = pl.BlockSpec(memory_space=pl.ANY)
    vmem = pl.BlockSpec(memory_space=pltpu.VMEM)
    count, wide = sources[0].shape
    held = [] if into is None else [into]
    return pl.pallas_call(
        functools.partial(place_kernel, quarters),
        out_shape=jax.ShapeDtypeStruct((count, 4 * wide), f32),
        in_specs=[pl.BlockSpec(memory_space=pltpu.SMEM)] + [hbm] * len(held) + [vmem] * len(sources),
        out_specs=hbm,
        scratch_shapes=[pltpu.SemaphoreType.DMA((len(quarters),))],
        input_output_aliases={1: 0} if held else {},
        compiler_params=pltpu.CompilerParams(vmem_limit_bytes=8 << 20),
        name="place",
    )(where, *held, *sources)


def swap(array, axis, bit):
    return lax.ppermute(array, axis, [(i, i ^ bit) for i in range(lax.axis_size(axis))])


def onward(array, axis):
    size = lax.axis_size(axis)
    return lax.ppermute(array, axis, [(i, (i + 2) % size) for i in range(size)])


def body(
    vectors,
    wear_freq,
    param_scale,
    row_angle,
    row_weight,
    entry_block,
    entry_row,
    entry_count,
    block_home,
):
    holders = lax.axis_size("rows")
    members = lax.axis_size("grp")
    vector_count = vectors.shape[0]
    blocks_here = vectors.shape[1] // BLK_P
    slots = entry_block.shape[0]
    capacity = slots // holders
    width = row_angle.shape[0]

    names = jnp.arange(block_home.shape[0], dtype=jnp.int32)
    stored = jnp.sum(
        jnp.where(entry_block[:, None] == names[None, :], block_home[None, :], 0), axis=1
    )
    slot_ids = jnp.arange(slots, dtype=jnp.int32)
    live = slot_ids < entry_count[0]
    holder = jnp.where(live, stored // blocks_here, -1)
    earlier = (holder[:, None] == holder[None, :]) & (slot_ids[None, :] < slot_ids[:, None])
    places = jnp.sum(earlier.astype(jnp.int32), axis=1)
    code = entry_row * blocks_here + stored % blocks_here
    target = jnp.where(live, holder * capacity + places, -1)
    room_ids = jnp.arange(holders * capacity, dtype=jnp.int32)
    wanted = (
        jnp.sum(jnp.where(target[None, :] == room_ids[:, None], code[None, :] + 1, 0), axis=1) - 1
    )
    wanted = wanted.reshape(holders, 1, capacity).astype(f32)

    angle_rows = jnp.stack(
        angle_pieces(row_angle.astype(f32)) + [row_weight.astype(f32)], axis=0
    )
    send = jnp.concatenate(
        [
            jnp.broadcast_to(angle_rows[None], (holders, PIECES - 1, width)),
            jnp.pad(wanted, ((0, 0), (0, 0), (0, width - capacity))),
        ],
        axis=1,
    ).astype(bf16)
    left = lax.all_to_all(send, "rows", split_axis=0, concat_axis=0, tiled=True)
    codes = left[:, PIECES - 1, :capacity].astype(jnp.int32).reshape(holders * capacity)

    freq = wear_freq.reshape(blocks_here, 1, BLK_P)
    scale = (param_scale.astype(f32) * (1.0 / math.sqrt(8.0 * BLK_P))).astype(bf16)
    scale = scale.reshape(blocks_here, 1, BLK_P)
    kind = lax.broadcasted_iota(jnp.int32, (1, PIECES, 1), 1)
    right = jnp.concatenate(
        [
            jnp.where(kind < PIECES - 2, freq, jnp.zeros_like(freq)),
            jnp.where(kind == PIECES - 2, scale, jnp.zeros_like(scale)),
        ],
        axis=2,
    )
    me = lax.axis_index("rows")
    core = lax.axis_index("grp") % 2
    side, position = me % 2, me // 2
    ring = holders // 2

    splits = 2 if ring % 2 == 0 else 1
    *far, far_jac = forward(
        codes, jnp.stack([position, 1 - side]), left, right, vectors, capacity, splits
    )
    far = [swap(array, "rows", 1) for array in far]
    near, near_jac = forward(codes, jnp.stack([position, side]), left, right, vectors, capacity, 1)
    each = ring // splits
    running = None
    for k in range(ring):
        own = near[k] + far[k // each][k % each]
        running = own if running is None else own + onward(running, "rows")
    outputs = running.astype(bf16)

    same, across = [outputs], [swap(outputs, "rows", 1)]
    for k in range(1, ring):
        outputs = onward(outputs, "rows")
        same.append(outputs)
        across.append(swap(outputs, "rows", 1))
    pieces = same + across

    def terms(first, here, pieces):
        where = jnp.stack([position, side, first])
        return backward(codes, where, near_jac, far_jac, pieces, blocks_here, here, capacity)

    half = blocks_here // 2
    wide = half // 2 * BLK_P
    given, pieces = terms((1 - core) * half, half, pieces)
    given = swap(given, "grp", 1)
    sums = []
    for chunk in range(2):
        kept, _ = terms(core * half + chunk * half // 2, half // 2, pieces)
        chunk_sum = kept + given[:, chunk * wide : (chunk + 1) * wide]
        bit = 2
        while bit < members:
            rounded = lax.reduce_precision(chunk_sum, 8, 7)
            sent = rounded.astype(bf16)
            codes, sent, sums = lax.optimization_barrier((codes, sent, sums))
            chunk_sum = rounded + swap(sent, "grp", bit).astype(f32)
            bit *= 2
        sums.append(chunk_sum)
    held = [(chunk_sum, swap(chunk_sum, "grp", 1)) for chunk_sum in sums]
    where = core.reshape(1)
    total = place(where, None, ((True, 0), (False, 0), (True, 1)), (*held[0], held[1][0]))
    return place(where, total, ((False, 1),), (held[1][1],))


def solution(mesh):
    return jax.shard_map(
        body,
        mesh=mesh,
        in_specs=(
            P(None, "rows"),
            P("rows"),
            P("rows"),
            P(("rows", "grp")),
            P(("rows", "grp")),
            P(("rows", "grp")),
            P(("rows", "grp")),
            P(("rows", "grp")),
            P(),
        ),
        out_specs=P(None, "rows"),
        check_vma=False,
    )
```

```python
import functools
import math

import jax
import jax.numpy as jnp
from jax import lax
from jax.experimental import pallas as pl
from jax.experimental.pallas import tpu as pltpu
from jax.sharding import PartitionSpec as P

BLK_R = 256
BLK_P = 512
PIECES = 8
RING = 8

f32 = jnp.float32
bf16 = jnp.bfloat16

COS_POLY = (
    1.4142134965678816,
    -6.978850988354285,
    5.7394611717976565,
    -1.8835629903409246,
    0.3106981920279389,
)
ROUNDER = 12582912.0


def turn_constants():
    constants = []
    rest = 1.0 / (2.0 * math.pi)
    for _ in range(3):
        mantissa, exponent = math.frexp(rest)
        constant = math.ldexp(round(mantissa * 256.0) / 256.0, exponent)
        constants.append(constant)
        rest -= constant
    return constants


def angle_pieces(angles):
    out = []
    for constant in turn_constants():
        exact = angles * constant
        top = lax.reduce_precision(exact, 8, 7)
        out += [top, exact - top]
    return out


def collect(codes, todo, start, places, wanted):
    def visit(step, found):
        todo[found] = start + step
        code = codes[start + step]
        return found + ((code >= 0) & wanted(code)).astype(jnp.int32)

    return lax.fori_loop(0, places, visit, 0)


def entry_cost(entries, vector_count):
    return pl.CostEstimate(flops=entries, bytes_accessed=vector_count, transcendentals=0)


def forward_kernel(blocks, capacity, codes, where, left, right, vectors, *refs):
    near, far, jac, todo, part, even, odd, sems = refs[-8:]
    spare = codes.shape[0]
    part[...] = jnp.zeros_like(part)
    start = 2 * capacity * where[0]
    found = collect(codes, todo, start, 2 * capacity, lambda code: True)
    steps = (found + 1) // 2

    def decode(place):
        code = codes[place]
        group = lax.div(place, capacity)
        away = jnp.where(lax.rem(group, 2) == where[1], 0, 1)
        return lax.rem(code, blocks), lax.div(code, blocks), group, away

    def make(buffer, place):
        block, row, group, _ = decode(place)
        angles = left[group, :, pl.ds(pl.multiple_of(row * BLK_R, BLK_R), BLK_R)]
        both = lax.dot_general(
            angles, right[block], (((0,), (0,)), ((), ())), preferred_element_type=f32
        )
        turns, weight = both[:, :BLK_P], both[:, BLK_P:]
        rest = turns - ((turns + ROUNDER) - ROUNDER)
        square = rest * rest
        root = COS_POLY[4] * square + COS_POLY[3]
        for k in (2, 1, 0):
            root = root * square + COS_POLY[k]
        buffer[...] = (weight * (root * root - 1.0)).astype(bf16)

    def apply(buffer, place, keep):
        block, row, _, away = decode(place)
        chosen = vectors[:, pl.ds(pl.multiple_of(block * BLK_P, BLK_P), BLK_P)]
        term = lax.dot_general(
            buffer[...], chosen, (((1,), (1,)), ((), ())), preferred_element_type=f32
        )
        if keep is not None:
            term = jnp.where(keep, term, 0.0)
        part[away, :, pl.ds(pl.multiple_of(row * BLK_R, BLK_R), BLK_R)] += term.T

    def save(buffer, parity, which, place):
        return pltpu.make_async_copy(buffer.at[parity], jac.at[place], sems.at[parity, which])

    def step(turn, before):
        parity = lax.rem(turn, 2)
        first = todo[2 * turn]
        paired = 2 * turn + 1 < found
        second = todo[jnp.where(paired, 2 * turn + 1, 2 * turn)]

        @pl.when(turn >= 2)
        def _():
            save(even, parity, 0, 0).wait()
            save(odd, parity, 1, 0).wait()

        apply(odd.at[1 - parity], before, turn > 0)
        make(even.at[parity], first)
        save(even, parity, 0, first).start()
        apply(even.at[parity], first, None)
        make(odd.at[parity], second)
        save(odd, parity, 1, jnp.where(paired, second, spare)).start()
        return second

    last = lax.fori_loop(0, steps, step, 0)

    @pl.when((found > 0) & (lax.rem(found, 2) == 0))
    def _():
        apply(odd.at[lax.rem(steps + 1, 2)], last, None)

    for back in (1, 2):
        @pl.when(steps >= back)
        def _():
            parity = lax.rem(steps + back, 2)
            save(even, parity, 0, 0).wait()
            save(odd, parity, 1, 0).wait()

    near[...] = part[0]
    far[...] = part[1]


def forward(codes, where, left, right, vectors, capacity, jac):
    _, _, width = left.shape
    blocks = right.shape[0]
    room = codes.shape[0]
    count = vectors.shape[0]
    vmem = pl.BlockSpec(memory_space=pltpu.VMEM)
    smem = pl.BlockSpec(memory_space=pltpu.SMEM)
    hbm = pl.BlockSpec(memory_space=pltpu.HBM)
    held = [] if jac is None else [jac]
    return pl.pallas_call(
        functools.partial(forward_kernel, blocks, capacity),
        out_shape=(jax.ShapeDtypeStruct((count, width), f32),) * 2
        + (pltpu.HBM((room + 1, BLK_R, BLK_P), bf16),),
        in_specs=[smem, smem, vmem, vmem, vmem] + [hbm] * len(held),
        out_specs=(vmem, vmem, hbm),
        scratch_shapes=[
            pltpu.SMEM((2 * capacity + 1,), jnp.int32),
            pltpu.VMEM((2, count, width), f32),
            pltpu.VMEM((2, BLK_R, BLK_P), bf16),
            pltpu.VMEM((2, BLK_R, BLK_P), bf16),
            pltpu.SemaphoreType.DMA((2, 2)),
        ],
        input_output_aliases={5: 2} if held else {},
        compiler_params=pltpu.CompilerParams(vmem_limit_bytes=16 << 20),
        cost_estimate=entry_cost(2 * capacity, count),
        name="forward",
    )(codes, where, left, right, vectors, *held)


def backward_kernel(blocks, capacity, ring, codes, where, jac, *refs):
    *pieces, out, gathered, todo, buffers, sems = refs
    here = out.shape[1] // BLK_P
    depth = buffers.shape[0]

    def wanted(code):
        block = lax.rem(code, blocks)
        return (block >= where[2]) & (block < where[2] + here)

    found = collect(codes, todo, 0, codes.shape[0], wanted)

    def load(turn):
        slot = lax.rem(turn, depth)
        return pltpu.make_async_copy(jac.at[todo[turn]], buffers.at[slot], sems.at[slot])

    def prime(turn, carry):
        load(turn).start()
        return carry

    lax.fori_loop(0, jnp.minimum(found, depth - 1), prime, 0)
    for k in range(len(pieces)):
        gathered[k] = pieces[k][...]
    out[...] = jnp.zeros_like(out)

    def step(turn, carry):
        @pl.when(turn + depth - 1 < found)
        def _():
            load(turn + depth - 1).start()

        place = todo[turn]
        code = codes[place]
        block, row = lax.rem(code, blocks) - where[2], lax.div(code, blocks)
        behind = lax.rem(where[0] - lax.div(place, 2 * capacity) + ring, ring)
        near = lax.rem(lax.div(place, capacity), 2) == where[1]
        piece = jnp.where(near, behind, ring + behind)
        chosen = gathered[piece, :, pl.ds(pl.multiple_of(row * BLK_R, BLK_R), BLK_R)]
        at = pl.ds(pl.multiple_of(block * BLK_P, BLK_P), BLK_P)
        slot = lax.rem(turn, depth)
        load(turn).wait()
        out[:, at] += jnp.dot(chosen, buffers[slot], preferred_element_type=f32)
        return carry

    lax.fori_loop(0, found, step, 0)


def joined_backward_kernel(blocks, capacity, ring, *refs):
    *inputs, gathered, out, todo, buffers, sems = refs
    backward_kernel(blocks, capacity, ring, *inputs, out, gathered, todo, buffers, sems)


def backward(codes, where, jac, pieces, blocks, here, capacity):
    joined = not isinstance(pieces, list)
    smem = pl.BlockSpec(memory_space=pltpu.SMEM)
    vmem = pl.BlockSpec(memory_space=pltpu.VMEM)
    hbm = pl.BlockSpec(memory_space=pl.ANY)
    sources = [pieces] if joined else pieces
    count, width = sources[0].shape[-2:]
    total = pieces.shape[0] if joined else len(pieces)
    terms = jax.ShapeDtypeStruct((count, here * BLK_P), f32)
    gathered = jax.ShapeDtypeStruct((total, count, width), bf16)
    kernel = joined_backward_kernel if joined else backward_kernel
    result = pl.pallas_call(
        functools.partial(kernel, blocks, capacity, total // 2),
        out_shape=terms if joined else (terms, gathered),
        in_specs=[smem, smem, hbm] + [vmem] * len(sources),
        out_specs=vmem if joined else (vmem, vmem),
        scratch_shapes=[
            pltpu.SMEM((codes.shape[0] + 1,), jnp.int32),
            pltpu.VMEM((RING, BLK_R, BLK_P), bf16),
            pltpu.SemaphoreType.DMA((RING,)),
        ],
        compiler_params=pltpu.CompilerParams(vmem_limit_bytes=36 << 20),
        cost_estimate=entry_cost(codes.shape[0] // 8, count),
        name="backward",
    )(codes, where, jac, *sources)
    return (result, pieces) if joined else result


def place_kernel(quarters, where, *refs):
    *sources, out, sems = refs
    sources = sources[-len(quarters) :]
    wide = sources[0].shape[1]
    copies = []
    for k, (mine, chunk) in enumerate(quarters):
        half = where[0] if mine else 1 - where[0]
        at = pl.ds(pl.multiple_of((2 * half + chunk) * wide, wide), wide)
        copies.append(pltpu.make_async_copy(sources[k], out.at[:, at], sems.at[k]))
    for copy in copies:
        copy.start()
    for copy in copies:
        copy.wait()


def place(where, into, quarters, sources):
    hbm = pl.BlockSpec(memory_space=pl.ANY)
    vmem = pl.BlockSpec(memory_space=pltpu.VMEM)
    count, wide = sources[0].shape
    held = [] if into is None else [into]
    return pl.pallas_call(
        functools.partial(place_kernel, quarters),
        out_shape=jax.ShapeDtypeStruct((count, 4 * wide), f32),
        in_specs=[pl.BlockSpec(memory_space=pltpu.SMEM)] + [hbm] * len(held) + [vmem] * len(sources),
        out_specs=hbm,
        scratch_shapes=[pltpu.SemaphoreType.DMA((len(quarters),))],
        input_output_aliases={1: 0} if held else {},
        compiler_params=pltpu.CompilerParams(vmem_limit_bytes=8 << 20),
        name="place",
    )(where, *held, *sources)


def swap(array, axis, bit):
    return lax.ppermute(array, axis, [(i, i ^ bit) for i in range(lax.axis_size(axis))])


def shift(array, axis, steps):
    size = lax.axis_size(axis)
    return lax.ppermute(array, axis, [(i, (i + 2 * steps) % size) for i in range(size)])


def body(
    vectors,
    wear_freq,
    param_scale,
    row_angle,
    row_weight,
    entry_block,
    entry_row,
    entry_count,
    block_home,
):
    holders = lax.axis_size("rows")
    members = lax.axis_size("grp")
    vector_count = vectors.shape[0]
    blocks_here = vectors.shape[1] // BLK_P
    slots = entry_block.shape[0]
    capacity = slots // holders
    width = row_angle.shape[0]

    names = jnp.arange(block_home.shape[0], dtype=jnp.int32)
    stored = jnp.sum(
        jnp.where(entry_block[:, None] == names[None, :], block_home[None, :], 0), axis=1
    )
    slot_ids = jnp.arange(slots, dtype=jnp.int32)
    live = slot_ids < entry_count[0]
    holder = jnp.where(live, stored // blocks_here, -1)
    earlier = (holder[:, None] == holder[None, :]) & (slot_ids[None, :] < slot_ids[:, None])
    places = jnp.sum(earlier.astype(jnp.int32), axis=1)
    code = entry_row * blocks_here + stored % blocks_here
    target = jnp.where(live, holder * capacity + places, -1)
    room_ids = jnp.arange(holders * capacity, dtype=jnp.int32)
    wanted = (
        jnp.sum(jnp.where(target[None, :] == room_ids[:, None], code[None, :] + 1, 0), axis=1) - 1
    )
    wanted = wanted.reshape(holders, 1, capacity).astype(f32)

    angle_rows = jnp.stack(
        angle_pieces(row_angle.astype(f32)) + [row_weight.astype(f32)], axis=0
    )
    send = jnp.concatenate(
        [
            jnp.broadcast_to(angle_rows[None], (holders, PIECES - 1, width)),
            jnp.pad(wanted, ((0, 0), (0, 0), (0, width - capacity))),
        ],
        axis=1,
    ).astype(bf16)
    left = lax.all_to_all(send, "rows", split_axis=0, concat_axis=0, tiled=True)
    codes = left[:, PIECES - 1, :capacity].astype(jnp.int32).reshape(holders * capacity)

    freq = wear_freq.reshape(blocks_here, 1, BLK_P)
    scale = (param_scale.astype(f32) * (1.0 / math.sqrt(8.0 * BLK_P))).astype(bf16)
    scale = scale.reshape(blocks_here, 1, BLK_P)
    kind = lax.broadcasted_iota(jnp.int32, (1, PIECES, 1), 1)
    right = jnp.concatenate(
        [
            jnp.where(kind < PIECES - 2, freq, jnp.zeros_like(freq)),
            jnp.where(kind == PIECES - 2, scale, jnp.zeros_like(scale)),
        ],
        axis=2,
    )
    me = lax.axis_index("rows")
    core = lax.axis_index("grp") % 2
    side, position = me % 2, me // 2
    ring = holders // 2

    jac = None
    waiting = []
    arrived = []
    for k in range(ring):
        where = jnp.stack([(position + 2 * ring - 1 - k) % ring, side])
        near, far, jac = forward(codes, where, left, right, vectors, capacity, jac)
        waiting.append((near, swap(far, "rows", 1)))
        if k > 0:
            before, got = waiting[k - 1]
            pair = before + got
            older = arrived[: ring - 3]
            codes, pair, older = lax.optimization_barrier((codes, pair, older))
            arrived = older + arrived[ring - 3 :]
            arrived.append(shift(pair, "rows", -k))
    near, got = waiting[-1]
    got, early = lax.optimization_barrier((got, arrived[:-1]))
    arrived = early + arrived[-1:]
    outputs = near + got
    for pair in arrived:
        outputs = outputs + pair
    outputs = outputs.astype(bf16)

    same = [outputs] + [shift(outputs, "rows", k) for k in range(1, ring)]
    pieces = same + [swap(piece, "rows", 1) for piece in same]

    def terms(first, here, pieces):
        where = jnp.stack([position, side, first])
        return backward(codes, where, jac, pieces, blocks_here, here, capacity)

    half = blocks_here // 2
    wide = half // 2 * BLK_P
    given, pieces = terms((1 - core) * half, half, pieces)
    given = swap(given, "grp", 1)
    sums = []
    for chunk in range(2):
        kept, _ = terms(core * half + chunk * half // 2, half // 2, pieces)
        chunk_sum = kept + given[:, chunk * wide : (chunk + 1) * wide]
        bit = 2
        while bit < members:
            rounded = lax.reduce_precision(chunk_sum, 8, 7)
            sent = rounded.astype(bf16)
            codes, sent, sums = lax.optimization_barrier((codes, sent, sums))
            chunk_sum = rounded + swap(sent, "grp", bit).astype(f32)
            bit *= 2
        sums.append(chunk_sum)
    held = [(chunk_sum, swap(chunk_sum, "grp", 1)) for chunk_sum in sums]
    where = core.reshape(1)
    total = place(where, None, ((True, 0), (False, 0), (True, 1)), (*held[0], held[1][0]))
    return place(where, total, ((False, 1),), (held[1][1],))


def solution(mesh):
    return jax.shard_map(
        body,
        mesh=mesh,
        in_specs=(
            P(None, "rows"),
            P("rows"),
            P("rows"),
            P(("rows", "grp")),
            P(("rows", "grp")),
            P(("rows", "grp")),
            P(("rows", "grp")),
            P(("rows", "grp")),
            P(),
        ),
        out_specs=P(None, "rows"),
        check_vma=False,
    )
```

```python
import functools
import math

import jax
import jax.numpy as jnp
from jax import lax
from jax.experimental import pallas as pl
from jax.experimental.pallas import tpu as pltpu
from jax.sharding import PartitionSpec as P

BLK_R = 256
BLK_P = 512
PIECES = 8
RING = 8

f32 = jnp.float32
bf16 = jnp.bfloat16

COS_POLY = (
    1.4142134965678816,
    -6.978850988354285,
    5.7394611717976565,
    -1.8835629903409246,
    0.3106981920279389,
)


def turn_constants():
    constants = []
    rest = 1.0 / (2.0 * math.pi)
    for _ in range(3):
        mantissa, exponent = math.frexp(rest)
        constant = math.ldexp(round(mantissa * 256.0) / 256.0, exponent)
        constants.append(constant)
        rest -= constant
    return constants


def angle_pieces(angles):
    out = []
    for constant in turn_constants():
        exact = angles * constant
        top = lax.reduce_precision(exact, 8, 7)
        out += [top, exact - top]
    return out


def collect(codes, todo, start, places, wanted):
    def visit(step, found):
        todo[found] = start + step
        code = codes[start + step]
        return found + ((code >= 0) & wanted(code)).astype(jnp.int32)

    return lax.fori_loop(0, places, visit, 0)


def entry_cost(entries, vector_count):
    return pl.CostEstimate(flops=entries, bytes_accessed=vector_count, transcendentals=0)


def forward_kernel(blocks, capacity, stage, codes, left, right, vectors, *refs):
    near, far, jac, todo, part, even, odd, sems = refs[-8:]
    spare = codes.shape[0]
    part[...] = jnp.zeros_like(part)
    start = 2 * capacity * stage
    found = collect(codes, todo, start, 2 * capacity, lambda code: True)
    steps = (found + 1) // 2

    def decode(place):
        code = codes[place]
        return lax.rem(code, blocks), lax.div(code, blocks), lax.div(place - start, capacity)

    def make(buffer, place):
        block, row, away = decode(place)
        angles = left[2 * stage + away, :, pl.ds(pl.multiple_of(row * BLK_R, BLK_R), BLK_R)]
        both = lax.dot_general(
            angles, right[block], (((0,), (0,)), ((), ())), preferred_element_type=f32
        )
        turns, weight = both[:, :BLK_P], both[:, BLK_P:]
        rest = turns - jnp.round(turns)
        square = rest * rest
        root = COS_POLY[4] * square + COS_POLY[3]
        for k in (2, 1, 0):
            root = root * square + COS_POLY[k]
        buffer[...] = (weight * (root * root - 1.0)).astype(bf16)

    def apply(buffer, place, keep):
        block, row, away = decode(place)
        chosen = vectors[:, pl.ds(pl.multiple_of(block * BLK_P, BLK_P), BLK_P)]
        term = lax.dot_general(
            buffer[...], chosen, (((1,), (1,)), ((), ())), preferred_element_type=f32
        )
        if keep is not None:
            term = jnp.where(keep, term, 0.0)
        part[away, :, pl.ds(pl.multiple_of(row * BLK_R, BLK_R), BLK_R)] += term.T

    def save(buffer, parity, which, place):
        return pltpu.make_async_copy(buffer.at[parity], jac.at[place], sems.at[parity, which])

    def step(turn, before):
        parity = lax.rem(turn, 2)
        first = todo[2 * turn]
        paired = 2 * turn + 1 < found
        second = todo[jnp.where(paired, 2 * turn + 1, 2 * turn)]

        @pl.when(turn >= 2)
        def _():
            save(even, parity, 0, 0).wait()
            save(odd, parity, 1, 0).wait()

        apply(odd.at[1 - parity], before, turn > 0)
        make(even.at[parity], first)
        save(even, parity, 0, first).start()
        apply(even.at[parity], first, None)
        make(odd.at[parity], second)
        save(odd, parity, 1, jnp.where(paired, second, spare)).start()
        return second

    last = lax.fori_loop(0, steps, step, todo[0])

    @pl.when((found > 0) & (lax.rem(found, 2) == 0))
    def _():
        apply(odd.at[lax.rem(steps + 1, 2)], last, None)

    for back in (1, 2):
        @pl.when(steps >= back)
        def _():
            parity = lax.rem(steps + back, 2)
            save(even, parity, 0, 0).wait()
            save(odd, parity, 1, 0).wait()

    near[...] = part[0]
    far[...] = part[1]


def forward(codes, stage, left, right, vectors, capacity, jac):
    width = left.shape[2]
    blocks = right.shape[0]
    room = codes.shape[0]
    count = vectors.shape[0]
    vmem = pl.BlockSpec(memory_space=pltpu.VMEM)
    smem = pl.BlockSpec(memory_space=pltpu.SMEM)
    hbm = pl.BlockSpec(memory_space=pltpu.HBM)
    held = [] if jac is None else [jac]
    return pl.pallas_call(
        functools.partial(forward_kernel, blocks, capacity, stage),
        out_shape=(jax.ShapeDtypeStruct((count, width), f32),) * 2
        + (pltpu.HBM((room + 1, BLK_R, BLK_P), bf16),),
        in_specs=[smem, vmem, vmem, vmem] + [hbm] * len(held),
        out_specs=(vmem, vmem, hbm),
        scratch_shapes=[
            pltpu.SMEM((2 * capacity + 1,), jnp.int32),
            pltpu.VMEM((2, count, width), f32),
            pltpu.VMEM((2, BLK_R, BLK_P), bf16),
            pltpu.VMEM((2, BLK_R, BLK_P), bf16),
            pltpu.SemaphoreType.DMA((2, 2)),
        ],
        input_output_aliases={4: 2} if held else {},
        compiler_params=pltpu.CompilerParams(vmem_limit_bytes=16 << 20),
        cost_estimate=entry_cost(2 * capacity, count),
        name="forward",
    )(codes, left, right, vectors, *held)


def backward_kernel(blocks, capacity, codes, first, jac, *refs):
    *pieces, out, gathered, todo, buffers, sems = refs
    here = out.shape[1] // BLK_P
    depth = buffers.shape[0]

    def wanted(code):
        block = lax.rem(code, blocks)
        return (block >= first[0]) & (block < first[0] + here)

    found = collect(codes, todo, 0, codes.shape[0], wanted)

    def load(turn):
        slot = lax.rem(turn, depth)
        return pltpu.make_async_copy(jac.at[todo[turn]], buffers.at[slot], sems.at[slot])

    def prime(turn, carry):
        load(turn).start()
        return carry

    lax.fori_loop(0, jnp.minimum(found, depth - 1), prime, 0)
    for k in range(len(pieces)):
        gathered[k] = pieces[k][...]
    out[...] = jnp.zeros_like(out)

    def step(turn, carry):
        @pl.when(turn + depth - 1 < found)
        def _():
            load(turn + depth - 1).start()

        place = todo[turn]
        code = codes[place]
        block, row = lax.rem(code, blocks) - first[0], lax.div(code, blocks)
        piece = lax.div(place, capacity)
        chosen = gathered[piece, :, pl.ds(pl.multiple_of(row * BLK_R, BLK_R), BLK_R)]
        at = pl.ds(pl.multiple_of(block * BLK_P, BLK_P), BLK_P)
        slot = lax.rem(turn, depth)
        load(turn).wait()
        out[:, at] += jnp.dot(chosen, buffers[slot], preferred_element_type=f32)
        return carry

    lax.fori_loop(0, found, step, 0)


def joined_backward_kernel(blocks, capacity, *refs):
    *inputs, gathered, out, todo, buffers, sems = refs
    backward_kernel(blocks, capacity, *inputs, out, gathered, todo, buffers, sems)


def backward(codes, first, jac, pieces, blocks, here, capacity):
    joined = not isinstance(pieces, list)
    smem = pl.BlockSpec(memory_space=pltpu.SMEM)
    vmem = pl.BlockSpec(memory_space=pltpu.VMEM)
    hbm = pl.BlockSpec(memory_space=pl.ANY)
    sources = [pieces] if joined else pieces
    count, width = sources[0].shape[-2:]
    total = pieces.shape[0] if joined else len(pieces)
    terms = jax.ShapeDtypeStruct((count, here * BLK_P), f32)
    gathered = jax.ShapeDtypeStruct((total, count, width), bf16)
    kernel = joined_backward_kernel if joined else backward_kernel
    result = pl.pallas_call(
        functools.partial(kernel, blocks, capacity),
        out_shape=terms if joined else (terms, gathered),
        in_specs=[smem, smem, hbm] + [vmem] * len(sources),
        out_specs=vmem if joined else (vmem, vmem),
        scratch_shapes=[
            pltpu.SMEM((codes.shape[0] + 1,), jnp.int32),
            pltpu.VMEM((RING, BLK_R, BLK_P), bf16),
            pltpu.SemaphoreType.DMA((RING,)),
        ],
        compiler_params=pltpu.CompilerParams(vmem_limit_bytes=36 << 20),
        cost_estimate=entry_cost(codes.shape[0] // 8, count),
        name="backward",
    )(codes, first, jac, *sources)
    return (result, pieces) if joined else result


def place_kernel(quarters, where, *refs):
    *sources, out, sems = refs
    sources = sources[-len(quarters) :]
    wide = sources[0].shape[1]
    copies = []
    for k, (mine, chunk) in enumerate(quarters):
        half = where[0] if mine else 1 - where[0]
        at = pl.ds(pl.multiple_of((2 * half + chunk) * wide, wide), wide)
        copies.append(pltpu.make_async_copy(sources[k], out.at[:, at], sems.at[k]))
    for copy in copies:
        copy.start()
    for copy in copies:
        copy.wait()


def place(where, into, quarters, sources):
    hbm = pl.BlockSpec(memory_space=pl.ANY)
    vmem = pl.BlockSpec(memory_space=pltpu.VMEM)
    count, wide = sources[0].shape
    held = [] if into is None else [into]
    return pl.pallas_call(
        functools.partial(place_kernel, quarters),
        out_shape=jax.ShapeDtypeStruct((count, 4 * wide), f32),
        in_specs=[pl.BlockSpec(memory_space=pltpu.SMEM)] + [hbm] * len(held) + [vmem] * len(sources),
        out_specs=hbm,
        scratch_shapes=[pltpu.SemaphoreType.DMA((len(quarters),))],
        input_output_aliases={1: 0} if held else {},
        compiler_params=pltpu.CompilerParams(vmem_limit_bytes=8 << 20),
        name="place",
    )(where, *held, *sources)


def swap(array, axis, bit):
    return lax.ppermute(array, axis, [(i, i ^ bit) for i in range(lax.axis_size(axis))])


def shift(array, axis, steps, bit=0):
    size = lax.axis_size(axis)
    return lax.ppermute(array, axis, [(i, (i + 2 * steps) % size ^ bit) for i in range(size)])


def body(
    vectors,
    wear_freq,
    param_scale,
    row_angle,
    row_weight,
    entry_block,
    entry_row,
    entry_count,
    block_home,
):
    holders = lax.axis_size("rows")
    members = lax.axis_size("grp")
    vector_count = vectors.shape[0]
    blocks_here = vectors.shape[1] // BLK_P
    slots = entry_block.shape[0]
    capacity = slots // holders
    width = row_angle.shape[0]

    names = jnp.arange(block_home.shape[0], dtype=jnp.int32)
    stored = jnp.sum(
        jnp.where(entry_block[:, None] == names[None, :], block_home[None, :], 0), axis=1
    )
    slot_ids = jnp.arange(slots, dtype=jnp.int32)
    live = slot_ids < entry_count[0]
    holder = jnp.where(live, stored // blocks_here, -1)
    earlier = (holder[:, None] == holder[None, :]) & (slot_ids[None, :] < slot_ids[:, None])
    places = jnp.sum(earlier.astype(jnp.int32), axis=1)
    code = entry_row * blocks_here + stored % blocks_here
    target = jnp.where(live, holder * capacity + places, -1)
    room_ids = jnp.arange(holders * capacity, dtype=jnp.int32)
    wanted = (
        jnp.sum(jnp.where(target[None, :] == room_ids[:, None], code[None, :] + 1, 0), axis=1) - 1
    )
    wanted = jnp.pad(wanted.astype(f32), (0, width - slots))

    mine = jnp.stack(
        angle_pieces(row_angle.astype(f32)) + [row_weight.astype(f32), wanted], axis=0
    ).astype(bf16)
    ring = holders // 2
    lefts = []
    for k in range(1, ring + 1):
        lefts.append(shift(mine, "rows", k) if k < ring else mine)
        lefts.append(shift(mine, "rows", k % ring, 1))
    left = lax.optimization_barrier(jnp.stack(lefts))
    me = lax.axis_index("rows")
    codes = lax.dynamic_slice(
        left, (0, PIECES - 1, me * capacity), (holders, 1, capacity)
    )
    codes = codes.astype(jnp.int32).reshape(holders * capacity)

    freq = wear_freq.reshape(blocks_here, 1, BLK_P)
    scale = (param_scale.astype(f32) * (1.0 / math.sqrt(8.0 * BLK_P))).astype(bf16)
    scale = scale.reshape(blocks_here, 1, BLK_P)
    kind = lax.broadcasted_iota(jnp.int32, (1, PIECES, 1), 1)
    right = jnp.concatenate(
        [
            jnp.where(kind < PIECES - 2, freq, jnp.zeros_like(freq)),
            jnp.where(kind == PIECES - 2, scale, jnp.zeros_like(scale)),
        ],
        axis=2,
    )
    core = lax.axis_index("grp") % 2

    jac = None
    waiting = []
    arrived = []
    for k in range(ring):
        near, far, jac = forward(codes, k, left, right, vectors, capacity, jac)
        waiting.append((near, swap(far, "rows", 1)))
        if k > 0:
            before, got = waiting[k - 1]
            pair = before + got
            older = arrived[: ring - 3]
            codes, pair, older = lax.optimization_barrier((codes, pair, older))
            arrived = older + arrived[ring - 3 :]
            arrived.append(shift(pair, "rows", -k))
    near, got = waiting[-1]
    got, early = lax.optimization_barrier((got, arrived[:-1]))
    arrived = early + arrived[-1:]
    outputs = near + got
    for pair in arrived:
        outputs = outputs + pair
    outputs = outputs.astype(bf16)

    same = [shift(outputs, "rows", k) for k in range(1, ring)] + [outputs]
    pieces = [piece for near in same for piece in (near, swap(near, "rows", 1))]

    def terms(first, pieces):
        return backward(codes, first.reshape(1), jac, pieces, blocks_here, quarter, capacity)

    quarter = blocks_here // 4
    sums = []
    for chunk in range(2):
        given, pieces = terms((2 * (1 - core) + chunk) * quarter, pieces)
        given = swap(given, "grp", 1)
        kept, pieces = terms((2 * core + chunk) * quarter, pieces)
        chunk_sum = kept + given
        bit = 2
        while bit < members:
            rounded = lax.reduce_precision(chunk_sum, 8, 7)
            sent = rounded.astype(bf16)
            codes, sent, sums = lax.optimization_barrier((codes, sent, sums))
            chunk_sum = rounded + swap(sent, "grp", bit).astype(f32)
            bit *= 2
        sums.append(chunk_sum)
    held = [(chunk_sum, swap(chunk_sum, "grp", 1)) for chunk_sum in sums]
    where = core.reshape(1)
    total = place(where, None, ((True, 0), (False, 0), (True, 1)), (*held[0], held[1][0]))
    return place(where, total, ((False, 1),), (held[1][1],))


def solution(mesh):
    return jax.shard_map(
        body,
        mesh=mesh,
        in_specs=(
            P(None, "rows"),
            P("rows"),
            P("rows"),
            P(("rows", "grp")),
            P(("rows", "grp")),
            P(("rows", "grp")),
            P(("rows", "grp")),
            P(("rows", "grp")),
            P(),
        ),
        out_specs=P(None, "rows"),
        check_vma=False,
    )
```

```python
import functools
import math

import jax
import jax.numpy as jnp
from jax import lax
from jax.experimental import pallas as pl
from jax.experimental.pallas import tpu as pltpu
from jax.sharding import PartitionSpec as P

BLK_R = 256
BLK_P = 512
PIECES = 8
RING = 8

f32 = jnp.float32
bf16 = jnp.bfloat16

COS_POLY = (
    1.4142134965678816,
    -6.978850988354285,
    5.7394611717976565,
    -1.8835629903409246,
    0.3106981920279389,
)


def turn_constants():
    constants = []
    rest = 1.0 / (2.0 * math.pi)
    for _ in range(3):
        mantissa, exponent = math.frexp(rest)
        constant = math.ldexp(round(mantissa * 256.0) / 256.0, exponent)
        constants.append(constant)
        rest -= constant
    return constants


def angle_pieces(angles):
    out = []
    for constant in turn_constants():
        exact = angles * constant
        top = lax.reduce_precision(exact, 8, 7)
        out += [top, exact - top]
    return out


def collect(codes, todo, start, places, low, high):
    def visit(step, found):
        todo[found] = start + step
        code = codes[start + step]
        return found + ((code >= low) & (code < high)).astype(jnp.int32)

    return lax.fori_loop(0, places, visit, 0, unroll=8 if places % 8 == 0 else 1)


def entry_cost(entries, vector_count):
    return pl.CostEstimate(flops=entries, bytes_accessed=vector_count, transcendentals=0)


def forward_kernel(blocks, capacity, codes, where, left, right, vectors, *refs):
    near, far, jac, todo, part, even, odd, sems = refs[-8:]
    spare = codes.shape[0]
    rows = left.shape[2] // BLK_R
    part[...] = jnp.zeros_like(part)
    start = 2 * capacity * where[0]
    found = collect(codes, todo, start, 2 * capacity, 0, blocks * rows)
    steps = (found + 1) // 2

    def decode(place):
        code = codes[place]
        group = lax.div(place, capacity)
        away = jnp.where(lax.rem(group, 2) == where[1], 0, 1)
        return lax.div(code, rows), lax.rem(code, rows), group, away

    def make(buffer, place):
        block, row, group, _ = decode(place)
        angles = left[group, :, pl.ds(pl.multiple_of(row * BLK_R, BLK_R), BLK_R)]
        both = lax.dot_general(
            angles, right[block], (((0,), (0,)), ((), ())), preferred_element_type=f32
        )
        turns, weight = both[:, :BLK_P], both[:, BLK_P:]
        rest = turns - jnp.round(turns)
        square = rest * rest
        root = COS_POLY[4] * square + COS_POLY[3]
        for k in (2, 1, 0):
            root = root * square + COS_POLY[k]
        buffer[...] = (weight * (root * root - 1.0)).astype(bf16)

    def apply(buffer, place, keep):
        block, row, _, away = decode(place)
        chosen = vectors[:, pl.ds(pl.multiple_of(block * BLK_P, BLK_P), BLK_P)]
        term = lax.dot_general(
            buffer[...], chosen, (((1,), (1,)), ((), ())), preferred_element_type=f32
        )
        if keep is not None:
            term = jnp.where(keep, term, 0.0)
        part[away, :, pl.ds(pl.multiple_of(row * BLK_R, BLK_R), BLK_R)] += term.T

    def save(buffer, parity, which, place):
        return pltpu.make_async_copy(buffer.at[parity], jac.at[place], sems.at[parity, which])

    def step(turn, before):
        parity = lax.rem(turn, 2)
        first = todo[2 * turn]
        paired = 2 * turn + 1 < found
        second = todo[jnp.where(paired, 2 * turn + 1, 2 * turn)]

        @pl.when(turn >= 2)
        def _():
            save(even, parity, 0, 0).wait()
            save(odd, parity, 1, 0).wait()

        apply(odd.at[1 - parity], before, turn > 0)
        make(even.at[parity], first)
        save(even, parity, 0, first).start()
        apply(even.at[parity], first, None)
        make(odd.at[parity], second)
        save(odd, parity, 1, jnp.where(paired, second, spare)).start()
        return second

    last = lax.fori_loop(0, steps, step, todo[0])

    @pl.when((found > 0) & (lax.rem(found, 2) == 0))
    def _():
        apply(odd.at[lax.rem(steps + 1, 2)], last, None)

    for back in (1, 2):
        @pl.when(steps >= back)
        def _():
            parity = lax.rem(steps + back, 2)
            save(even, parity, 0, 0).wait()
            save(odd, parity, 1, 0).wait()

    near[...] = part[0]
    far[...] = part[1]


def forward(codes, where, left, right, vectors, capacity, jac):
    _, _, width = left.shape
    blocks = right.shape[0]
    room = codes.shape[0]
    count = vectors.shape[0]
    vmem = pl.BlockSpec(memory_space=pltpu.VMEM)
    smem = pl.BlockSpec(memory_space=pltpu.SMEM)
    hbm = pl.BlockSpec(memory_space=pltpu.HBM)
    held = [] if jac is None else [jac]
    return pl.pallas_call(
        functools.partial(forward_kernel, blocks, capacity),
        out_shape=(jax.ShapeDtypeStruct((count, width), f32),) * 2
        + (pltpu.HBM((room + 1, BLK_R, BLK_P), bf16),),
        in_specs=[smem, smem, vmem, vmem, vmem] + [hbm] * len(held),
        out_specs=(vmem, vmem, hbm),
        scratch_shapes=[
            pltpu.SMEM((2 * capacity + 1,), jnp.int32),
            pltpu.VMEM((2, count, width), f32),
            pltpu.VMEM((2, BLK_R, BLK_P), bf16),
            pltpu.VMEM((2, BLK_R, BLK_P), bf16),
            pltpu.SemaphoreType.DMA((2, 2)),
        ],
        input_output_aliases={5: 2} if held else {},
        compiler_params=pltpu.CompilerParams(vmem_limit_bytes=16 << 20),
        cost_estimate=entry_cost(2 * capacity, count),
        name="forward",
    )(codes, where, left, right, vectors, *held)


def backward_kernel(capacity, ring, codes, where, jac, *refs):
    *pieces, out, gathered, todo, buffers, sems = refs
    here = out.shape[1] // BLK_P
    depth = buffers.shape[0]

    rows = gathered.shape[2] // BLK_R
    found = collect(codes, todo, 0, codes.shape[0], where[2] * rows, (where[2] + here) * rows)

    def load(turn):
        slot = lax.rem(turn, depth)
        return pltpu.make_async_copy(jac.at[todo[turn]], buffers.at[slot], sems.at[slot])

    def prime(turn, carry):
        load(turn).start()
        return carry

    lax.fori_loop(0, jnp.minimum(found, depth - 1), prime, 0)
    for k in range(len(pieces)):
        gathered[k] = pieces[k][...]
    out[...] = jnp.zeros_like(out)

    def step(turn, carry):
        @pl.when(turn + depth - 1 < found)
        def _():
            load(turn + depth - 1).start()

        place = todo[turn]
        code = codes[place]
        block, row = lax.div(code, rows) - where[2], lax.rem(code, rows)
        behind = lax.rem(where[0] - lax.div(place, 2 * capacity) + ring, ring)
        near = lax.rem(lax.div(place, capacity), 2) == where[1]
        piece = jnp.where(near, behind, ring + behind)
        chosen = gathered[piece, :, pl.ds(pl.multiple_of(row * BLK_R, BLK_R), BLK_R)]
        at = pl.ds(pl.multiple_of(block * BLK_P, BLK_P), BLK_P)
        slot = lax.rem(turn, depth)
        load(turn).wait()
        out[:, at] += jnp.dot(chosen, buffers[slot], preferred_element_type=f32)
        return carry

    lax.fori_loop(0, found, step, 0)


def joined_backward_kernel(capacity, ring, *refs):
    *inputs, gathered, out, todo, buffers, sems = refs
    backward_kernel(capacity, ring, *inputs, out, gathered, todo, buffers, sems)


def backward(codes, where, jac, pieces, here, capacity):
    joined = not isinstance(pieces, list)
    smem = pl.BlockSpec(memory_space=pltpu.SMEM)
    vmem = pl.BlockSpec(memory_space=pltpu.VMEM)
    hbm = pl.BlockSpec(memory_space=pl.ANY)
    sources = [pieces] if joined else pieces
    count, width = sources[0].shape[-2:]
    total = pieces.shape[0] if joined else len(pieces)
    terms = jax.ShapeDtypeStruct((count, here * BLK_P), f32)
    gathered = jax.ShapeDtypeStruct((total, count, width), bf16)
    kernel = joined_backward_kernel if joined else backward_kernel
    result = pl.pallas_call(
        functools.partial(kernel, capacity, total // 2),
        out_shape=terms if joined else (terms, gathered),
        in_specs=[smem, smem, hbm] + [vmem] * len(sources),
        out_specs=vmem if joined else (vmem, vmem),
        scratch_shapes=[
            pltpu.SMEM((codes.shape[0] + 1,), jnp.int32),
            pltpu.VMEM((RING, BLK_R, BLK_P), bf16),
            pltpu.SemaphoreType.DMA((RING,)),
        ],
        compiler_params=pltpu.CompilerParams(vmem_limit_bytes=36 << 20),
        cost_estimate=entry_cost(codes.shape[0] // 8, count),
        name="backward",
    )(codes, where, jac, *sources)
    return (result, pieces) if joined else result


def place_kernel(quarters, where, *refs):
    *sources, out, sems = refs
    sources = sources[-len(quarters) :]
    wide = sources[0].shape[1]
    copies = []
    for k, (mine, chunk) in enumerate(quarters):
        half = where[0] if mine else 1 - where[0]
        at = pl.ds(pl.multiple_of((2 * half + chunk) * wide, wide), wide)
        copies.append(pltpu.make_async_copy(sources[k], out.at[:, at], sems.at[k]))
    for copy in copies:
        copy.start()
    for copy in copies:
        copy.wait()


def place(where, into, quarters, sources):
    hbm = pl.BlockSpec(memory_space=pl.ANY)
    vmem = pl.BlockSpec(memory_space=pltpu.VMEM)
    count, wide = sources[0].shape
    held = [] if into is None else [into]
    return pl.pallas_call(
        functools.partial(place_kernel, quarters),
        out_shape=jax.ShapeDtypeStruct((count, 4 * wide), f32),
        in_specs=[pl.BlockSpec(memory_space=pltpu.SMEM)] + [hbm] * len(held) + [vmem] * len(sources),
        out_specs=hbm,
        scratch_shapes=[pltpu.SemaphoreType.DMA((len(quarters),))],
        input_output_aliases={1: 0} if held else {},
        compiler_params=pltpu.CompilerParams(vmem_limit_bytes=8 << 20),
        name="place",
    )(where, *held, *sources)


def swap(array, axis, bit):
    return lax.ppermute(array, axis, [(i, i ^ bit) for i in range(lax.axis_size(axis))])


def shift(array, axis, steps):
    size = lax.axis_size(axis)
    return lax.ppermute(array, axis, [(i, (i + 2 * steps) % size) for i in range(size)])


def body(
    vectors,
    wear_freq,
    param_scale,
    row_angle,
    row_weight,
    entry_block,
    entry_row,
    entry_count,
    block_home,
):
    holders = lax.axis_size("rows")
    members = lax.axis_size("grp")
    vector_count = vectors.shape[0]
    blocks_here = vectors.shape[1] // BLK_P
    slots = entry_block.shape[0]
    capacity = slots // holders
    width = row_angle.shape[0]

    names = jnp.arange(block_home.shape[0], dtype=jnp.int32)
    stored = jnp.sum(
        jnp.where(entry_block[:, None] == names[None, :], block_home[None, :], 0), axis=1
    )
    slot_ids = jnp.arange(slots, dtype=jnp.int32)
    live = slot_ids < entry_count[0]
    holder = jnp.where(live, stored // blocks_here, -1)
    earlier = (holder[:, None] == holder[None, :]) & (slot_ids[None, :] < slot_ids[:, None])
    places = jnp.sum(earlier.astype(jnp.int32), axis=1)
    code = stored % blocks_here * (width // BLK_R) + entry_row
    target = jnp.where(live, holder * capacity + places, -1)
    room_ids = jnp.arange(holders * capacity, dtype=jnp.int32)
    wanted = (
        jnp.sum(jnp.where(target[None, :] == room_ids[:, None], code[None, :] + 1, 0), axis=1) - 1
    )
    wanted = wanted.reshape(holders, 1, capacity).astype(f32)

    angle_rows = jnp.stack(
        angle_pieces(row_angle.astype(f32)) + [row_weight.astype(f32)], axis=0
    )
    send = jnp.concatenate(
        [
            jnp.broadcast_to(angle_rows[None], (holders, PIECES - 1, width)),
            jnp.pad(wanted, ((0, 0), (0, 0), (0, width - capacity))),
        ],
        axis=1,
    ).astype(bf16)
    left = lax.all_to_all(send, "rows", split_axis=0, concat_axis=0, tiled=True)
    codes = left[:, PIECES - 1, :capacity].astype(jnp.int32).reshape(holders * capacity)

    freq = wear_freq.reshape(blocks_here, 1, BLK_P)
    scale = (param_scale.astype(f32) * (1.0 / math.sqrt(8.0 * BLK_P))).astype(bf16)
    scale = scale.reshape(blocks_here, 1, BLK_P)
    kind = lax.broadcasted_iota(jnp.int32, (1, PIECES, 1), 1)
    right = jnp.concatenate(
        [
            jnp.where(kind < PIECES - 2, freq, jnp.zeros_like(freq)),
            jnp.where(kind == PIECES - 2, scale, jnp.zeros_like(scale)),
        ],
        axis=2,
    )
    me = lax.axis_index("rows")
    core = lax.axis_index("grp") % 2
    side, position = me % 2, me // 2
    ring = holders // 2

    jac = None
    waiting = []
    arrived = []
    for k in range(ring):
        where = jnp.stack([(position + 2 * ring - 1 - k) % ring, side])
        near, far, jac = forward(codes, where, left, right, vectors, capacity, jac)
        waiting.append((near, swap(far, "rows", 1)))
        if k > 0:
            before, got = waiting[k - 1]
            pair = before + got
            older = arrived[: ring - 3]
            codes, pair, older = lax.optimization_barrier((codes, pair, older))
            arrived = older + arrived[ring - 3 :]
            arrived.append(shift(pair, "rows", -k))
    near, got = waiting[-1]
    got, early = lax.optimization_barrier((got, arrived[:-1]))
    arrived = early + arrived[-1:]
    outputs = near + got
    for pair in arrived:
        outputs = outputs + pair
    outputs = outputs.astype(bf16)

    same = [outputs] + [shift(outputs, "rows", k) for k in range(1, ring)]
    pieces = same + [swap(piece, "rows", 1) for piece in same]

    def terms(first, pieces):
        where = jnp.stack([position, side, first])
        return backward(codes, where, jac, pieces, quarter, capacity)

    quarter = blocks_here // 4
    sums = []
    for chunk in range(2):
        given, pieces = terms((2 * (1 - core) + chunk) * quarter, pieces)
        given = swap(given, "grp", 1)
        kept, pieces = terms((2 * core + chunk) * quarter, pieces)
        chunk_sum = kept + given
        bit = 2
        while bit < members:
            rounded = lax.reduce_precision(chunk_sum, 8, 7)
            sent = rounded.astype(bf16)
            codes, sent, sums = lax.optimization_barrier((codes, sent, sums))
            chunk_sum = rounded + swap(sent, "grp", bit).astype(f32)
            bit *= 2
        sums.append(chunk_sum)
    held = [(chunk_sum, swap(chunk_sum, "grp", 1)) for chunk_sum in sums]
    where = core.reshape(1)
    total = place(where, None, ((True, 0), (False, 0), (True, 1)), (*held[0], held[1][0]))
    return place(where, total, ((False, 1),), (held[1][1],))


def solution(mesh):
    return jax.shard_map(
        body,
        mesh=mesh,
        in_specs=(
            P(None, "rows"),
            P("rows"),
            P("rows"),
            P(("rows", "grp")),
            P(("rows", "grp")),
            P(("rows", "grp")),
            P(("rows", "grp")),
            P(("rows", "grp")),
            P(),
        ),
        out_specs=P(None, "rows"),
        check_vma=False,
    )
```

```python
import functools
import math

import jax
import jax.numpy as jnp
from jax import lax
from jax.experimental import pallas as pl
from jax.experimental.pallas import tpu as pltpu
from jax.sharding import PartitionSpec as P

BLK_R = 256
BLK_P = 512
PIECES = 8
RING = 8

f32 = jnp.float32
bf16 = jnp.bfloat16

COS_POLY = (
    1.4142134965678816,
    -6.978850988354285,
    5.7394611717976565,
    -1.8835629903409246,
    0.3106981920279389,
)


def turn_constants():
    constants = []
    rest = 1.0 / (2.0 * math.pi)
    for _ in range(3):
        mantissa, exponent = math.frexp(rest)
        constant = math.ldexp(round(mantissa * 256.0) / 256.0, exponent)
        constants.append(constant)
        rest -= constant
    return constants


def angle_pieces(angles):
    out = []
    for constant in turn_constants():
        exact = angles * constant
        top = lax.reduce_precision(exact, 8, 7)
        out += [top, exact - top]
    return out


def collect(codes, todo, start, places, low, high):
    def visit(step, found):
        todo[found] = start + step
        code = codes[start + step]
        return found + ((code >= low) & (code < high)).astype(jnp.int32)

    return lax.fori_loop(0, places, visit, 0, unroll=8 if places % 8 == 0 else 1)


def entry_cost(entries, vector_count):
    return pl.CostEstimate(flops=entries, bytes_accessed=vector_count, transcendentals=0)


def forward_kernel(blocks, capacity, codes, where, left, right, vectors, *refs):
    near, far, jac, todo, part, even, odd, chosen, sems, chosen_sems = refs[-10:]
    spare = codes.shape[0]
    rows = left.shape[2] // BLK_R
    part[...] = jnp.zeros_like(part)
    start = 2 * capacity * where[0]
    found = collect(codes, todo, start, 2 * capacity, 0, blocks * rows)
    steps = (found + 1) // 2

    def decode(place):
        code = codes[place]
        group = lax.div(place, capacity)
        away = jnp.where(lax.rem(group, 2) == where[1], 0, 1)
        return lax.div(code, rows), lax.rem(code, rows), group, away

    def make(buffer, place):
        block, row, group, _ = decode(place)
        angles = left[group, :, pl.ds(pl.multiple_of(row * BLK_R, BLK_R), BLK_R)]
        both = lax.dot_general(
            angles, right[block], (((0,), (0,)), ((), ())), preferred_element_type=f32
        )
        turns, weight = both[:, :BLK_P], both[:, BLK_P:]
        rest = turns - jnp.round(turns)
        square = rest * rest
        root = COS_POLY[4] * square + COS_POLY[3]
        for k in (2, 1, 0):
            root = root * square + COS_POLY[k]
        buffer[...] = (weight * (root * root - 1.0)).astype(bf16)

    def fetch(turn, which, place):
        slot = lax.rem(turn, 3)
        at = pl.ds(pl.multiple_of(decode(place)[0] * BLK_P, BLK_P), BLK_P)
        return pltpu.make_async_copy(
            vectors.at[:, at], chosen.at[slot, which], chosen_sems.at[slot, which]
        )

    def apply(buffer, place, turn, which, keep):
        _, row, _, away = decode(place)
        term = lax.dot_general(
            buffer[...],
            chosen[lax.rem(turn, 3), which],
            (((1,), (1,)), ((), ())),
            preferred_element_type=f32,
        )
        if keep is not None:
            term = jnp.where(keep, term, 0.0)
        part[away, :, pl.ds(pl.multiple_of(row * BLK_R, BLK_R), BLK_R)] += term.T

    def save(buffer, parity, which, place):
        return pltpu.make_async_copy(buffer.at[parity], jac.at[place], sems.at[parity, which])

    def entries(turn):
        paired = 2 * turn + 1 < found
        return todo[2 * turn], todo[jnp.where(paired, 2 * turn + 1, 2 * turn)], paired

    def fetch_both(turn):
        first, second, _ = entries(turn)
        fetch(turn, 0, first).start()
        fetch(turn, 1, second).start()

    @pl.when(steps > 0)
    def _():
        fetch_both(0)

    def step(turn, before):
        parity = lax.rem(turn, 2)
        first, second, paired = entries(turn)

        @pl.when(turn + 1 < steps)
        def _():
            fetch_both(turn + 1)

        @pl.when(turn >= 2)
        def _():
            save(even, parity, 0, 0).wait()
            save(odd, parity, 1, 0).wait()

        fetch(turn, 0, first).wait()
        fetch(turn, 1, second).wait()
        apply(odd.at[1 - parity], before, turn + 2, 1, turn > 0)
        make(even.at[parity], first)
        save(even, parity, 0, first).start()
        apply(even.at[parity], first, turn, 0, None)
        make(odd.at[parity], second)
        save(odd, parity, 1, jnp.where(paired, second, spare)).start()
        return second

    last = lax.fori_loop(0, steps, step, todo[0])

    @pl.when((found > 0) & (lax.rem(found, 2) == 0))
    def _():
        apply(odd.at[lax.rem(steps + 1, 2)], last, steps + 2, 1, None)

    for back in (1, 2):
        @pl.when(steps >= back)
        def _():
            parity = lax.rem(steps + back, 2)
            save(even, parity, 0, 0).wait()
            save(odd, parity, 1, 0).wait()

    near[...] = part[0]
    far[...] = part[1]


def forward(codes, where, left, right, vectors, capacity, jac):
    _, _, width = left.shape
    blocks = right.shape[0]
    room = codes.shape[0]
    count = vectors.shape[0]
    vmem = pl.BlockSpec(memory_space=pltpu.VMEM)
    smem = pl.BlockSpec(memory_space=pltpu.SMEM)
    hbm = pl.BlockSpec(memory_space=pltpu.HBM)
    held = [] if jac is None else [jac]
    return pl.pallas_call(
        functools.partial(forward_kernel, blocks, capacity),
        out_shape=(jax.ShapeDtypeStruct((count, width), f32),) * 2
        + (pltpu.HBM((room + 1, BLK_R, BLK_P), bf16),),
        in_specs=[smem, smem, vmem, vmem, hbm] + [hbm] * len(held),
        out_specs=(vmem, vmem, hbm),
        scratch_shapes=[
            pltpu.SMEM((2 * capacity + 1,), jnp.int32),
            pltpu.VMEM((2, count, width), f32),
            pltpu.VMEM((2, BLK_R, BLK_P), bf16),
            pltpu.VMEM((2, BLK_R, BLK_P), bf16),
            pltpu.VMEM((3, 2, count, BLK_P), bf16),
            pltpu.SemaphoreType.DMA((2, 2)),
            pltpu.SemaphoreType.DMA((3, 2)),
        ],
        input_output_aliases={5: 2} if held else {},
        compiler_params=pltpu.CompilerParams(vmem_limit_bytes=16 << 20),
        cost_estimate=entry_cost(2 * capacity, count),
        name="forward",
    )(codes, where, left, right, vectors, *held)


def backward_kernel(capacity, ring, codes, where, jac, *refs):
    *pieces, out, gathered, todo, buffers, sems = refs
    here = out.shape[1] // BLK_P
    depth = buffers.shape[0]

    rows = gathered.shape[2] // BLK_R
    found = collect(codes, todo, 0, codes.shape[0], where[2] * rows, (where[2] + here) * rows)

    def load(turn):
        slot = lax.rem(turn, depth)
        return pltpu.make_async_copy(jac.at[todo[turn]], buffers.at[slot], sems.at[slot])

    def prime(turn, carry):
        load(turn).start()
        return carry

    lax.fori_loop(0, jnp.minimum(found, depth - 1), prime, 0)
    for k in range(len(pieces)):
        gathered[k] = pieces[k][...]
    out[...] = jnp.zeros_like(out)

    def step(turn, carry):
        @pl.when(turn + depth - 1 < found)
        def _():
            load(turn + depth - 1).start()

        place = todo[turn]
        code = codes[place]
        block, row = lax.div(code, rows) - where[2], lax.rem(code, rows)
        behind = lax.rem(where[0] - lax.div(place, 2 * capacity) + ring, ring)
        near = lax.rem(lax.div(place, capacity), 2) == where[1]
        piece = jnp.where(near, behind, ring + behind)
        chosen = gathered[piece, :, pl.ds(pl.multiple_of(row * BLK_R, BLK_R), BLK_R)]
        at = pl.ds(pl.multiple_of(block * BLK_P, BLK_P), BLK_P)
        slot = lax.rem(turn, depth)
        load(turn).wait()
        out[:, at] += jnp.dot(chosen, buffers[slot], preferred_element_type=f32)
        return carry

    lax.fori_loop(0, found, step, 0)


def joined_backward_kernel(capacity, ring, *refs):
    *inputs, gathered, out, todo, buffers, sems = refs
    backward_kernel(capacity, ring, *inputs, out, gathered, todo, buffers, sems)


def backward(codes, where, jac, pieces, here, capacity):
    joined = not isinstance(pieces, list)
    smem = pl.BlockSpec(memory_space=pltpu.SMEM)
    vmem = pl.BlockSpec(memory_space=pltpu.VMEM)
    hbm = pl.BlockSpec(memory_space=pl.ANY)
    sources = [pieces] if joined else pieces
    count, width = sources[0].shape[-2:]
    total = pieces.shape[0] if joined else len(pieces)
    terms = jax.ShapeDtypeStruct((count, here * BLK_P), f32)
    gathered = jax.ShapeDtypeStruct((total, count, width), bf16)
    kernel = joined_backward_kernel if joined else backward_kernel
    result = pl.pallas_call(
        functools.partial(kernel, capacity, total // 2),
        out_shape=terms if joined else (terms, gathered),
        in_specs=[smem, smem, hbm] + [vmem] * len(sources),
        out_specs=vmem if joined else (vmem, vmem),
        scratch_shapes=[
            pltpu.SMEM((codes.shape[0] + 1,), jnp.int32),
            pltpu.VMEM((RING, BLK_R, BLK_P), bf16),
            pltpu.SemaphoreType.DMA((RING,)),
        ],
        compiler_params=pltpu.CompilerParams(vmem_limit_bytes=36 << 20),
        cost_estimate=entry_cost(codes.shape[0] // 8, count),
        name="backward",
    )(codes, where, jac, *sources)
    return (result, pieces) if joined else result


def place_kernel(quarters, where, *refs):
    *sources, out, sems = refs
    sources = sources[-len(quarters) :]
    wide = sources[0].shape[1]
    copies = []
    for k, (mine, chunk) in enumerate(quarters):
        half = where[0] if mine else 1 - where[0]
        at = pl.ds(pl.multiple_of((2 * half + chunk) * wide, wide), wide)
        copies.append(pltpu.make_async_copy(sources[k], out.at[:, at], sems.at[k]))
    for copy in copies:
        copy.start()
    for copy in copies:
        copy.wait()


def place(where, into, quarters, sources):
    hbm = pl.BlockSpec(memory_space=pl.ANY)
    vmem = pl.BlockSpec(memory_space=pltpu.VMEM)
    count, wide = sources[0].shape
    held = [] if into is None else [into]
    return pl.pallas_call(
        functools.partial(place_kernel, quarters),
        out_shape=jax.ShapeDtypeStruct((count, 4 * wide), f32),
        in_specs=[pl.BlockSpec(memory_space=pltpu.SMEM)] + [hbm] * len(held) + [vmem] * len(sources),
        out_specs=hbm,
        scratch_shapes=[pltpu.SemaphoreType.DMA((len(quarters),))],
        input_output_aliases={1: 0} if held else {},
        compiler_params=pltpu.CompilerParams(vmem_limit_bytes=8 << 20),
        name="place",
    )(where, *held, *sources)


def swap(array, axis, bit):
    return lax.ppermute(array, axis, [(i, i ^ bit) for i in range(lax.axis_size(axis))])


def shift(array, axis, steps):
    size = lax.axis_size(axis)
    return lax.ppermute(array, axis, [(i, (i + 2 * steps) % size) for i in range(size)])


def body(
    vectors,
    wear_freq,
    param_scale,
    row_angle,
    row_weight,
    entry_block,
    entry_row,
    entry_count,
    block_home,
):
    holders = lax.axis_size("rows")
    members = lax.axis_size("grp")
    vector_count = vectors.shape[0]
    blocks_here = vectors.shape[1] // BLK_P
    slots = entry_block.shape[0]
    capacity = slots // holders
    width = row_angle.shape[0]

    names = jnp.arange(block_home.shape[0], dtype=jnp.int32)
    stored = jnp.sum(
        jnp.where(entry_block[:, None] == names[None, :], block_home[None, :], 0), axis=1
    )
    slot_ids = jnp.arange(slots, dtype=jnp.int32)
    live = slot_ids < entry_count[0]
    holder = jnp.where(live, stored // blocks_here, -1)
    earlier = (holder[:, None] == holder[None, :]) & (slot_ids[None, :] < slot_ids[:, None])
    places = jnp.sum(earlier.astype(jnp.int32), axis=1)
    code = stored % blocks_here * (width // BLK_R) + entry_row
    target = jnp.where(live, holder * capacity + places, -1)
    room_ids = jnp.arange(holders * capacity, dtype=jnp.int32)
    wanted = (
        jnp.sum(jnp.where(target[None, :] == room_ids[:, None], code[None, :] + 1, 0), axis=1) - 1
    )
    wanted = wanted.reshape(holders, 1, capacity).astype(f32)

    angle_rows = jnp.stack(
        angle_pieces(row_angle.astype(f32)) + [row_weight.astype(f32)], axis=0
    )
    send = jnp.concatenate(
        [
            jnp.broadcast_to(angle_rows[None], (holders, PIECES - 1, width)),
            jnp.pad(wanted, ((0, 0), (0, 0), (0, width - capacity))),
        ],
        axis=1,
    ).astype(bf16)
    left = lax.all_to_all(send, "rows", split_axis=0, concat_axis=0, tiled=True)
    codes = left[:, PIECES - 1, :capacity].astype(jnp.int32).reshape(holders * capacity)

    freq = wear_freq.reshape(blocks_here, 1, BLK_P)
    scale = (param_scale.astype(f32) * (1.0 / math.sqrt(8.0 * BLK_P))).astype(bf16)
    scale = scale.reshape(blocks_here, 1, BLK_P)
    kind = lax.broadcasted_iota(jnp.int32, (1, PIECES, 1), 1)
    right = jnp.concatenate(
        [
            jnp.where(kind < PIECES - 2, freq, jnp.zeros_like(freq)),
            jnp.where(kind == PIECES - 2, scale, jnp.zeros_like(scale)),
        ],
        axis=2,
    )
    me = lax.axis_index("rows")
    core = lax.axis_index("grp") % 2
    vectors = pltpu.with_memory_space_constraint(vectors, pltpu.HBM)
    side, position = me % 2, me // 2
    ring = holders // 2

    jac = None
    waiting = []
    arrived = []
    for k in range(ring):
        where = jnp.stack([(position + 2 * ring - 1 - k) % ring, side])
        near, far, jac = forward(codes, where, left, right, vectors, capacity, jac)
        waiting.append((near, swap(far, "rows", 1)))
        if k > 0:
            before, got = waiting[k - 1]
            pair = before + got
            older = arrived[: ring - 3]
            codes, pair, older = lax.optimization_barrier((codes, pair, older))
            arrived = older + arrived[ring - 3 :]
            arrived.append(shift(pair, "rows", -k))
    near, got = waiting[-1]
    got, early = lax.optimization_barrier((got, arrived[:-1]))
    arrived = early + arrived[-1:]
    outputs = near + got
    for pair in arrived:
        outputs = outputs + pair
    outputs = outputs.astype(bf16)

    same = [outputs] + [shift(outputs, "rows", k) for k in range(1, ring)]
    pieces = same + [swap(piece, "rows", 1) for piece in same]

    def terms(first, pieces):
        where = jnp.stack([position, side, first])
        return backward(codes, where, jac, pieces, quarter, capacity)

    quarter = blocks_here // 4
    sums = []
    for chunk in range(2):
        given, pieces = terms((2 * (1 - core) + chunk) * quarter, pieces)
        given = swap(given, "grp", 1)
        kept, pieces = terms((2 * core + chunk) * quarter, pieces)
        chunk_sum = kept + given
        bit = 2
        while bit < members:
            rounded = lax.reduce_precision(chunk_sum, 8, 7)
            sent = rounded.astype(bf16)
            codes, sent, sums = lax.optimization_barrier((codes, sent, sums))
            chunk_sum = rounded + swap(sent, "grp", bit).astype(f32)
            bit *= 2
        sums.append(chunk_sum)
    held = [(chunk_sum, swap(chunk_sum, "grp", 1)) for chunk_sum in sums]
    where = core.reshape(1)
    total = place(where, None, ((True, 0), (False, 0), (True, 1)), (*held[0], held[1][0]))
    return place(where, total, ((False, 1),), (held[1][1],))


def solution(mesh):
    return jax.shard_map(
        body,
        mesh=mesh,
        in_specs=(
            P(None, "rows"),
            P("rows"),
            P("rows"),
            P(("rows", "grp")),
            P(("rows", "grp")),
            P(("rows", "grp")),
            P(("rows", "grp")),
            P(("rows", "grp")),
            P(),
        ),
        out_specs=P(None, "rows"),
        check_vma=False,
    )
```

```python
import functools
import math

import jax
import jax.numpy as jnp
from jax import lax
from jax.experimental import pallas as pl
from jax.experimental.pallas import tpu as pltpu
from jax.sharding import PartitionSpec as P

BLK_R = 256
BLK_P = 512
PIECES = 8
RING = 8

f32 = jnp.float32
bf16 = jnp.bfloat16

COS_POLY = (
    1.4142134965678816,
    -6.978850988354285,
    5.7394611717976565,
    -1.8835629903409246,
    0.3106981920279389,
)


def turn_constants():
    constants = []
    rest = 1.0 / (2.0 * math.pi)
    for _ in range(3):
        mantissa, exponent = math.frexp(rest)
        constant = math.ldexp(round(mantissa * 256.0) / 256.0, exponent)
        constants.append(constant)
        rest -= constant
    return constants


def angle_pieces(angles):
    out = []
    for constant in turn_constants():
        exact = angles * constant
        top = lax.reduce_precision(exact, 8, 7)
        out += [top, exact - top]
    return out


def collect(codes, todo, start, places, low, high):
    def visit(step, found):
        todo[found] = start + step
        code = codes[start + step]
        return found + ((code >= low) & (code < high)).astype(jnp.int32)

    return lax.fori_loop(0, places, visit, 0, unroll=8 if places % 8 == 0 else 1)


def entry_cost(entries, vector_count):
    return pl.CostEstimate(flops=entries, bytes_accessed=vector_count, transcendentals=0)


def forward_kernel(blocks, capacity, codes, where, left, right, vectors, *refs):
    near, far, jac, todo, columns, part, even, odd, sems = refs[-9:]
    spare = codes.shape[0]
    rows = left.shape[2] // BLK_R
    part[...] = jnp.zeros_like(part)
    start = 2 * capacity * where[0]
    found = collect(codes, todo, start, 2 * capacity, 0, blocks * rows)
    for k in range(2):
        for at in range(0, left.shape[2], 128):
            lanes = left[2 * where[0] + k, :, at : at + 128]
            columns[k, at : at + 128, :] = lanes.astype(f32).T.astype(bf16)
    steps = (found + 1) // 2

    def decode(place):
        code = codes[place]
        group = lax.div(place, capacity)
        away = jnp.where(lax.rem(group, 2) == where[1], 0, 1)
        return lax.div(code, rows), lax.rem(code, rows), group, away

    def make(buffer, place):
        block, row, group, _ = decode(place)
        at = pl.ds(pl.multiple_of(row * BLK_R, BLK_R), BLK_R)
        both = jnp.dot(
            columns[lax.rem(group, 2), at, :], right[block], preferred_element_type=f32
        )
        turns, weight = both[:, :BLK_P], both[:, BLK_P:]
        rest = turns - jnp.round(turns)
        square = rest * rest
        root = COS_POLY[4] * square + COS_POLY[3]
        for k in (2, 1, 0):
            root = root * square + COS_POLY[k]
        buffer[...] = (weight * (root * root - 1.0)).astype(bf16)

    def apply(buffer, place, keep):
        block, row, _, away = decode(place)
        chosen = vectors[:, pl.ds(pl.multiple_of(block * BLK_P, BLK_P), BLK_P)]
        term = lax.dot_general(
            buffer[...], chosen, (((1,), (1,)), ((), ())), preferred_element_type=f32
        )
        if keep is not None:
            term = jnp.where(keep, term, 0.0)
        part[away, :, pl.ds(pl.multiple_of(row * BLK_R, BLK_R), BLK_R)] += term.T

    def save(buffer, parity, which, place):
        return pltpu.make_async_copy(buffer.at[parity], jac.at[place], sems.at[parity, which])

    def step(turn, before):
        parity = lax.rem(turn, 2)
        first = todo[2 * turn]
        paired = 2 * turn + 1 < found
        second = todo[jnp.where(paired, 2 * turn + 1, 2 * turn)]

        @pl.when(turn >= 2)
        def _():
            save(even, parity, 0, 0).wait()
            save(odd, parity, 1, 0).wait()

        apply(odd.at[1 - parity], before, turn > 0)
        make(even.at[parity], first)
        save(even, parity, 0, first).start()
        apply(even.at[parity], first, None)
        make(odd.at[parity], second)
        save(odd, parity, 1, jnp.where(paired, second, spare)).start()
        return second

    last = lax.fori_loop(0, steps, step, todo[0])

    @pl.when((found > 0) & (lax.rem(found, 2) == 0))
    def _():
        apply(odd.at[lax.rem(steps + 1, 2)], last, None)

    for back in (1, 2):
        @pl.when(steps >= back)
        def _():
            parity = lax.rem(steps + back, 2)
            save(even, parity, 0, 0).wait()
            save(odd, parity, 1, 0).wait()

    near[...] = part[0]
    far[...] = part[1]


def forward(codes, where, left, right, vectors, capacity, jac):
    _, _, width = left.shape
    blocks = right.shape[0]
    room = codes.shape[0]
    count = vectors.shape[0]
    vmem = pl.BlockSpec(memory_space=pltpu.VMEM)
    smem = pl.BlockSpec(memory_space=pltpu.SMEM)
    hbm = pl.BlockSpec(memory_space=pltpu.HBM)
    held = [] if jac is None else [jac]
    return pl.pallas_call(
        functools.partial(forward_kernel, blocks, capacity),
        out_shape=(jax.ShapeDtypeStruct((count, width), f32),) * 2
        + (pltpu.HBM((room + 1, BLK_R, BLK_P), bf16),),
        in_specs=[smem, smem, vmem, vmem, vmem] + [hbm] * len(held),
        out_specs=(vmem, vmem, hbm),
        scratch_shapes=[
            pltpu.SMEM((2 * capacity + 1,), jnp.int32),
            pltpu.VMEM((2, width, PIECES), bf16),
            pltpu.VMEM((2, count, width), f32),
            pltpu.VMEM((2, BLK_R, BLK_P), bf16),
            pltpu.VMEM((2, BLK_R, BLK_P), bf16),
            pltpu.SemaphoreType.DMA((2, 2)),
        ],
        input_output_aliases={5: 2} if held else {},
        compiler_params=pltpu.CompilerParams(vmem_limit_bytes=16 << 20),
        cost_estimate=entry_cost(2 * capacity, count),
        name="forward",
    )(codes, where, left, right, vectors, *held)


def backward_kernel(capacity, ring, codes, where, jac, *refs):
    *pieces, out, gathered, todo, buffers, sems = refs
    here = out.shape[1] // BLK_P
    depth = buffers.shape[0]

    rows = gathered.shape[2] // BLK_R
    found = collect(codes, todo, 0, codes.shape[0], where[2] * rows, (where[2] + here) * rows)

    def load(turn):
        slot = lax.rem(turn, depth)
        return pltpu.make_async_copy(jac.at[todo[turn]], buffers.at[slot], sems.at[slot])

    def prime(turn, carry):
        load(turn).start()
        return carry

    lax.fori_loop(0, jnp.minimum(found, depth - 1), prime, 0)
    for k in range(len(pieces)):
        gathered[k] = pieces[k][...]
    out[...] = jnp.zeros_like(out)

    def step(turn, carry):
        @pl.when(turn + depth - 1 < found)
        def _():
            load(turn + depth - 1).start()

        place = todo[turn]
        code = codes[place]
        block, row = lax.div(code, rows) - where[2], lax.rem(code, rows)
        behind = lax.rem(where[0] - lax.div(place, 2 * capacity) + ring, ring)
        near = lax.rem(lax.div(place, capacity), 2) == where[1]
        piece = jnp.where(near, behind, ring + behind)
        chosen = gathered[piece, :, pl.ds(pl.multiple_of(row * BLK_R, BLK_R), BLK_R)]
        at = pl.ds(pl.multiple_of(block * BLK_P, BLK_P), BLK_P)
        slot = lax.rem(turn, depth)
        load(turn).wait()
        out[:, at] += jnp.dot(chosen, buffers[slot], preferred_element_type=f32)
        return carry

    lax.fori_loop(0, found, step, 0)


def joined_backward_kernel(capacity, ring, *refs):
    *inputs, gathered, out, todo, buffers, sems = refs
    backward_kernel(capacity, ring, *inputs, out, gathered, todo, buffers, sems)


def backward(codes, where, jac, pieces, here, capacity):
    joined = not isinstance(pieces, list)
    smem = pl.BlockSpec(memory_space=pltpu.SMEM)
    vmem = pl.BlockSpec(memory_space=pltpu.VMEM)
    hbm = pl.BlockSpec(memory_space=pl.ANY)
    sources = [pieces] if joined else pieces
    count, width = sources[0].shape[-2:]
    total = pieces.shape[0] if joined else len(pieces)
    terms = jax.ShapeDtypeStruct((count, here * BLK_P), f32)
    gathered = jax.ShapeDtypeStruct((total, count, width), bf16)
    kernel = joined_backward_kernel if joined else backward_kernel
    result = pl.pallas_call(
        functools.partial(kernel, capacity, total // 2),
        out_shape=terms if joined else (terms, gathered),
        in_specs=[smem, smem, hbm] + [vmem] * len(sources),
        out_specs=vmem if joined else (vmem, vmem),
        scratch_shapes=[
            pltpu.SMEM((codes.shape[0] + 1,), jnp.int32),
            pltpu.VMEM((RING, BLK_R, BLK_P), bf16),
            pltpu.SemaphoreType.DMA((RING,)),
        ],
        compiler_params=pltpu.CompilerParams(vmem_limit_bytes=36 << 20),
        cost_estimate=entry_cost(codes.shape[0] // 8, count),
        name="backward",
    )(codes, where, jac, *sources)
    return (result, pieces) if joined else result


def place_kernel(quarters, addends, where, *refs):
    *sources, out, sums, sems = refs
    sources = sources[-addends * len(quarters) :]
    wide = sums.shape[2]
    copies = []
    for k, (mine, chunk) in enumerate(quarters):
        total = sources[addends * k][...].astype(f32)
        for source in sources[addends * k + 1 : addends * (k + 1)]:
            total = total + source[...].astype(f32)
        sums[k] = total
        half = where[0] if mine else 1 - where[0]
        at = pl.ds(pl.multiple_of((2 * half + chunk) * wide, wide), wide)
        copies.append(pltpu.make_async_copy(sums.at[k], out.at[:, at], sems.at[k]))
        copies[-1].start()
    for copy in copies:
        copy.wait()


def place(where, into, quarters, groups):
    hbm = pl.BlockSpec(memory_space=pl.ANY)
    vmem = pl.BlockSpec(memory_space=pltpu.VMEM)
    sources = [array for group in groups for array in group]
    count, wide = sources[0].shape
    held = [] if into is None else [into]
    return pl.pallas_call(
        functools.partial(place_kernel, quarters, len(groups[0])),
        out_shape=jax.ShapeDtypeStruct((count, 4 * wide), f32),
        in_specs=[pl.BlockSpec(memory_space=pltpu.SMEM)] + [hbm] * len(held) + [vmem] * len(sources),
        out_specs=hbm,
        scratch_shapes=[
            pltpu.VMEM((len(quarters), count, wide), f32),
            pltpu.SemaphoreType.DMA((len(quarters),)),
        ],
        input_output_aliases={1: 0} if held else {},
        compiler_params=pltpu.CompilerParams(vmem_limit_bytes=10 << 20),
        name="place",
    )(where, *held, *sources)


def swap(array, axis, bit):
    return lax.ppermute(array, axis, [(i, i ^ bit) for i in range(lax.axis_size(axis))])


def shift(array, axis, steps):
    size = lax.axis_size(axis)
    return lax.ppermute(array, axis, [(i, (i + 2 * steps) % size) for i in range(size)])


def body(
    vectors,
    wear_freq,
    param_scale,
    row_angle,
    row_weight,
    entry_block,
    entry_row,
    entry_count,
    block_home,
):
    holders = lax.axis_size("rows")
    members = lax.axis_size("grp")
    vector_count = vectors.shape[0]
    blocks_here = vectors.shape[1] // BLK_P
    slots = entry_block.shape[0]
    capacity = slots // holders
    width = row_angle.shape[0]

    names = jnp.arange(block_home.shape[0], dtype=jnp.int32)
    stored = jnp.sum(
        jnp.where(entry_block[:, None] == names[None, :], block_home[None, :], 0), axis=1
    )
    slot_ids = jnp.arange(slots, dtype=jnp.int32)
    live = slot_ids < entry_count[0]
    holder = jnp.where(live, stored // blocks_here, -1)
    earlier = (holder[:, None] == holder[None, :]) & (slot_ids[None, :] < slot_ids[:, None])
    places = jnp.sum(earlier.astype(jnp.int32), axis=1)
    code = stored % blocks_here * (width // BLK_R) + entry_row
    target = jnp.where(live, holder * capacity + places, -1)
    room_ids = jnp.arange(holders * capacity, dtype=jnp.int32)
    wanted = (
        jnp.sum(jnp.where(target[None, :] == room_ids[:, None], code[None, :] + 1, 0), axis=1) - 1
    )
    wanted = wanted.reshape(holders, 1, capacity).astype(f32)

    angle_rows = jnp.stack(
        angle_pieces(row_angle.astype(f32)) + [row_weight.astype(f32)], axis=0
    )
    send = jnp.concatenate(
        [
            jnp.broadcast_to(angle_rows[None], (holders, PIECES - 1, width)),
            jnp.pad(wanted, ((0, 0), (0, 0), (0, width - capacity))),
        ],
        axis=1,
    ).astype(bf16)
    left = lax.all_to_all(send, "rows", split_axis=0, concat_axis=0, tiled=True)
    codes = left[:, PIECES - 1, :capacity].astype(jnp.int32).reshape(holders * capacity)

    freq = wear_freq.reshape(blocks_here, 1, BLK_P)
    scale = (param_scale.astype(f32) * (1.0 / math.sqrt(8.0 * BLK_P))).astype(bf16)
    scale = scale.reshape(blocks_here, 1, BLK_P)
    kind = lax.broadcasted_iota(jnp.int32, (1, PIECES, 1), 1)
    right = jnp.concatenate(
        [
            jnp.where(kind < PIECES - 2, freq, jnp.zeros_like(freq)),
            jnp.where(kind == PIECES - 2, scale, jnp.zeros_like(scale)),
        ],
        axis=2,
    )
    me = lax.axis_index("rows")
    core = lax.axis_index("grp") % 2
    side, position = me % 2, me // 2
    ring = holders // 2

    jac = None
    waiting = []
    arrived = []
    for k in range(ring):
        where = jnp.stack([(position + 2 * ring - 1 - k) % ring, side])
        near, far, jac = forward(codes, where, left, right, vectors, capacity, jac)
        waiting.append((near, swap(far, "rows", 1)))
        if k > 0:
            before, got = waiting[k - 1]
            pair = before + got
            older = arrived[: ring - 3]
            codes, pair, older = lax.optimization_barrier((codes, pair, older))
            arrived = older + arrived[ring - 3 :]
            arrived.append(shift(pair, "rows", -k))
    near, got = waiting[-1]
    got, early = lax.optimization_barrier((got, arrived[:-1]))
    arrived = early + arrived[-1:]
    outputs = near + got
    for pair in arrived:
        outputs = outputs + pair
    outputs = outputs.astype(bf16)

    same = [outputs] + [shift(outputs, "rows", k) for k in range(1, ring)]
    pieces = same + [swap(piece, "rows", 1) for piece in same]

    def terms(first, pieces):
        where = jnp.stack([position, side, first])
        return backward(codes, where, jac, pieces, quarter, capacity)

    quarter = blocks_here // 4
    pairs = []
    sums = []
    for chunk in range(2):
        given, pieces = terms((2 * (1 - core) + chunk) * quarter, pieces)
        given = swap(given, "grp", 1)
        kept, pieces = terms((2 * core + chunk) * quarter, pieces)
        chunk_sum = kept + given
        bit = 2
        pair = (chunk_sum, jnp.zeros_like(chunk_sum))
        while bit < members:
            rounded = lax.reduce_precision(chunk_sum, 8, 7)
            sent = rounded.astype(bf16)
            codes, sent, sums = lax.optimization_barrier((codes, sent, sums))
            pair = (sent, swap(sent, "grp", bit))
            chunk_sum = rounded + pair[1].astype(f32)
            bit *= 2
        sums.append(chunk_sum)
        pairs.append(pair)
    where = core.reshape(1)
    early = place(where, None, ((True, 0), (False, 0)), ((sums[0],), (swap(sums[0], "grp", 1),)))
    last = pairs[1]
    across = tuple(swap(array, "grp", 1) for array in last)
    return place(where, early, ((True, 1), (False, 1)), (last, across))


def solution(mesh):
    return jax.shard_map(
        body,
        mesh=mesh,
        in_specs=(
            P(None, "rows"),
            P("rows"),
            P("rows"),
            P(("rows", "grp")),
            P(("rows", "grp")),
            P(("rows", "grp")),
            P(("rows", "grp")),
            P(("rows", "grp")),
            P(),
        ),
        out_specs=P(None, "rows"),
        check_vma=False,
    )
```

```python
import functools
import math

import jax
import jax.numpy as jnp
from jax import lax
from jax.experimental import pallas as pl
from jax.experimental.pallas import tpu as pltpu
from jax.sharding import PartitionSpec as P

BLK_R = 256
BLK_P = 512
PIECES = 8
RING = 8

f32 = jnp.float32
bf16 = jnp.bfloat16

COS_POLY = (
    1.4142134965678816,
    -6.978850988354285,
    5.7394611717976565,
    -1.8835629903409246,
    0.3106981920279389,
)


def turn_constants():
    constants = []
    rest = 1.0 / (2.0 * math.pi)
    for _ in range(3):
        mantissa, exponent = math.frexp(rest)
        constant = math.ldexp(round(mantissa * 256.0) / 256.0, exponent)
        constants.append(constant)
        rest -= constant
    return constants


def angle_pieces(angles):
    out = []
    for constant in turn_constants():
        exact = angles * constant
        top = lax.reduce_precision(exact, 8, 7)
        out += [top, exact - top]
    return out


def collect(codes, todo, start, places, low, high):
    def visit(step, found):
        todo[found] = start + step
        code = codes[start + step]
        return found + ((code >= low) & (code < high)).astype(jnp.int32)

    return lax.fori_loop(0, places, visit, 0, unroll=8 if places % 8 == 0 else 1)


def entry_cost(entries, vector_count):
    return pl.CostEstimate(flops=entries, bytes_accessed=vector_count, transcendentals=0)


def forward_kernel(blocks, capacity, codes, where, left, right, vectors, *refs):
    near, far, jac, todo, columns, part, even, odd, sems = refs[-9:]
    spare = codes.shape[0]
    rows = left.shape[2] // BLK_R
    part[...] = jnp.zeros_like(part)
    start = 2 * capacity * where[0]
    found = collect(codes, todo, start, 2 * capacity, 0, blocks * rows)
    for k in range(2):
        for at in range(0, left.shape[2], 128):
            lanes = left[2 * where[0] + k, :, at : at + 128]
            columns[k, at : at + 128, :] = lanes.astype(f32).T.astype(bf16)
    steps = (found + 1) // 2

    def decode(place):
        code = codes[place]
        group = lax.div(place, capacity)
        away = jnp.where(lax.rem(group, 2) == where[1], 0, 1)
        return lax.div(code, rows), lax.rem(code, rows), group, away

    def make(buffer, place):
        block, row, group, _ = decode(place)
        at = pl.ds(pl.multiple_of(row * BLK_R, BLK_R), BLK_R)
        both = jnp.dot(
            columns[lax.rem(group, 2), at, :], right[block], preferred_element_type=f32
        )
        turns, weight = both[:, :BLK_P], both[:, BLK_P:]
        rest = turns - jnp.round(turns)
        square = rest * rest
        root = COS_POLY[4] * square + COS_POLY[3]
        for k in (2, 1, 0):
            root = root * square + COS_POLY[k]
        buffer[...] = (weight * (root * root - 1.0)).astype(bf16)

    def apply(buffer, place, keep):
        block, row, _, away = decode(place)
        chosen = vectors[:, pl.ds(pl.multiple_of(block * BLK_P, BLK_P), BLK_P)]
        term = lax.dot_general(
            buffer[...], chosen, (((1,), (1,)), ((), ())), preferred_element_type=f32
        )
        if keep is not None:
            term = jnp.where(keep, term, 0.0)
        part[away, :, pl.ds(pl.multiple_of(row * BLK_R, BLK_R), BLK_R)] += term.T

    def save(buffer, parity, which, place):
        return pltpu.make_async_copy(buffer.at[parity], jac.at[place], sems.at[parity, which])

    def step(turn, before):
        parity = lax.rem(turn, 2)
        first = todo[2 * turn]
        paired = 2 * turn + 1 < found
        second = todo[jnp.where(paired, 2 * turn + 1, 2 * turn)]

        @pl.when(turn >= 2)
        def _():
            save(even, parity, 0, 0).wait()
            save(odd, parity, 1, 0).wait()

        apply(odd.at[1 - parity], before, turn > 0)
        make(even.at[parity], first)
        save(even, parity, 0, first).start()
        apply(even.at[parity], first, None)
        make(odd.at[parity], second)
        save(odd, parity, 1, jnp.where(paired, second, spare)).start()
        return second

    last = lax.fori_loop(0, steps, step, todo[0])

    @pl.when((found > 0) & (lax.rem(found, 2) == 0))
    def _():
        apply(odd.at[lax.rem(steps + 1, 2)], last, None)

    for back in (1, 2):
        @pl.when(steps >= back)
        def _():
            parity = lax.rem(steps + back, 2)
            save(even, parity, 0, 0).wait()
            save(odd, parity, 1, 0).wait()

    near[...] = part[0]
    far[...] = part[1]


def forward(codes, where, left, right, vectors, capacity, jac):
    _, _, width = left.shape
    blocks = right.shape[0]
    room = codes.shape[0]
    count = vectors.shape[0]
    vmem = pl.BlockSpec(memory_space=pltpu.VMEM)
    smem = pl.BlockSpec(memory_space=pltpu.SMEM)
    hbm = pl.BlockSpec(memory_space=pltpu.HBM)
    held = [] if jac is None else [jac]
    return pl.pallas_call(
        functools.partial(forward_kernel, blocks, capacity),
        out_shape=(jax.ShapeDtypeStruct((count, width), f32),) * 2
        + (pltpu.HBM((room + 1, BLK_R, BLK_P), bf16),),
        in_specs=[smem, smem, vmem, vmem, vmem] + [hbm] * len(held),
        out_specs=(vmem, vmem, hbm),
        scratch_shapes=[
            pltpu.SMEM((2 * capacity + 1,), jnp.int32),
            pltpu.VMEM((2, width, PIECES), bf16),
            pltpu.VMEM((2, count, width), f32),
            pltpu.VMEM((2, BLK_R, BLK_P), bf16),
            pltpu.VMEM((2, BLK_R, BLK_P), bf16),
            pltpu.SemaphoreType.DMA((2, 2)),
        ],
        input_output_aliases={5: 2} if held else {},
        compiler_params=pltpu.CompilerParams(vmem_limit_bytes=16 << 20),
        cost_estimate=entry_cost(2 * capacity, count),
        name="forward",
    )(codes, where, left, right, vectors, *held)


def backward_kernel(capacity, ring, codes, where, jac, *refs):
    *pieces, out, gathered, todo, buffers, sems = refs
    here = out.shape[1] // BLK_P
    depth = buffers.shape[0]

    rows = gathered.shape[2] // BLK_R
    found = collect(codes, todo, 0, codes.shape[0], where[2] * rows, (where[2] + here) * rows)

    def load(turn):
        slot = lax.rem(turn, depth)
        return pltpu.make_async_copy(jac.at[todo[turn]], buffers.at[slot], sems.at[slot])

    def prime(turn, carry):
        load(turn).start()
        return carry

    lax.fori_loop(0, jnp.minimum(found, depth - 1), prime, 0)
    for k in range(len(pieces)):
        gathered[k] = pieces[k][...]
    out[...] = jnp.zeros_like(out)

    def step(turn, carry):
        @pl.when(turn + depth - 1 < found)
        def _():
            load(turn + depth - 1).start()

        place = todo[turn]
        code = codes[place]
        block, row = lax.div(code, rows) - where[2], lax.rem(code, rows)
        behind = lax.rem(where[0] - lax.div(place, 2 * capacity) + ring, ring)
        near = lax.rem(lax.div(place, capacity), 2) == where[1]
        piece = jnp.where(near, behind, ring + behind)
        chosen = gathered[piece, :, pl.ds(pl.multiple_of(row * BLK_R, BLK_R), BLK_R)]
        at = pl.ds(pl.multiple_of(block * BLK_P, BLK_P), BLK_P)
        slot = lax.rem(turn, depth)
        load(turn).wait()
        out[:, at] += jnp.dot(chosen, buffers[slot], preferred_element_type=f32)
        return carry

    lax.fori_loop(0, found, step, 0)


def joined_backward_kernel(capacity, ring, *refs):
    *inputs, gathered, out, todo, buffers, sems = refs
    backward_kernel(capacity, ring, *inputs, out, gathered, todo, buffers, sems)


def backward(codes, where, jac, pieces, here, capacity):
    joined = not isinstance(pieces, list)
    smem = pl.BlockSpec(memory_space=pltpu.SMEM)
    vmem = pl.BlockSpec(memory_space=pltpu.VMEM)
    hbm = pl.BlockSpec(memory_space=pl.ANY)
    sources = [pieces] if joined else pieces
    count, width = sources[0].shape[-2:]
    total = pieces.shape[0] if joined else len(pieces)
    terms = jax.ShapeDtypeStruct((count, here * BLK_P), f32)
    gathered = jax.ShapeDtypeStruct((total, count, width), bf16)
    kernel = joined_backward_kernel if joined else backward_kernel
    result = pl.pallas_call(
        functools.partial(kernel, capacity, total // 2),
        out_shape=terms if joined else (terms, gathered),
        in_specs=[smem, smem, hbm] + [vmem] * len(sources),
        out_specs=vmem if joined else (vmem, vmem),
        scratch_shapes=[
            pltpu.SMEM((codes.shape[0] + 1,), jnp.int32),
            pltpu.VMEM((RING, BLK_R, BLK_P), bf16),
            pltpu.SemaphoreType.DMA((RING,)),
        ],
        compiler_params=pltpu.CompilerParams(vmem_limit_bytes=36 << 20),
        cost_estimate=entry_cost(codes.shape[0] // 8, count),
        name="backward",
    )(codes, where, jac, *sources)
    return (result, pieces) if joined else result


def place_kernel(quarters, addends, where, *refs):
    *sources, out, sums, sems = refs
    sources = sources[-addends * len(quarters) :]
    wide = sums.shape[2]
    copies = []
    for k, (mine, chunk) in enumerate(quarters):
        total = sources[addends * k][...].astype(f32)
        for source in sources[addends * k + 1 : addends * (k + 1)]:
            total = total + source[...].astype(f32)
        sums[k] = total
        half = where[0] if mine else 1 - where[0]
        at = pl.ds(pl.multiple_of((2 * half + chunk) * wide, wide), wide)
        copies.append(pltpu.make_async_copy(sums.at[k], out.at[:, at], sems.at[k]))
        copies[-1].start()
    for copy in copies:
        copy.wait()


def place(where, into, quarters, groups):
    hbm = pl.BlockSpec(memory_space=pl.ANY)
    vmem = pl.BlockSpec(memory_space=pltpu.VMEM)
    sources = [array for group in groups for array in group]
    count, wide = sources[0].shape
    held = [] if into is None else [into]
    return pl.pallas_call(
        functools.partial(place_kernel, quarters, len(groups[0])),
        out_shape=jax.ShapeDtypeStruct((count, 4 * wide), f32),
        in_specs=[pl.BlockSpec(memory_space=pltpu.SMEM)] + [hbm] * len(held) + [vmem] * len(sources),
        out_specs=hbm,
        scratch_shapes=[
            pltpu.VMEM((len(quarters), count, wide), f32),
            pltpu.SemaphoreType.DMA((len(quarters),)),
        ],
        input_output_aliases={1: 0} if held else {},
        compiler_params=pltpu.CompilerParams(vmem_limit_bytes=10 << 20),
        name="place",
    )(where, *held, *sources)


def swap(array, axis, bit):
    return lax.ppermute(array, axis, [(i, i ^ bit) for i in range(lax.axis_size(axis))])


def shift(array, axis, steps):
    size = lax.axis_size(axis)
    return lax.ppermute(array, axis, [(i, (i + 2 * steps) % size) for i in range(size)])


def body(
    vectors,
    wear_freq,
    param_scale,
    row_angle,
    row_weight,
    entry_block,
    entry_row,
    entry_count,
    block_home,
):
    holders = lax.axis_size("rows")
    members = lax.axis_size("grp")
    vector_count = vectors.shape[0]
    blocks_here = vectors.shape[1] // BLK_P
    slots = entry_block.shape[0]
    capacity = slots // holders
    width = row_angle.shape[0]

    names = jnp.arange(block_home.shape[0], dtype=jnp.int32)
    stored = jnp.sum(
        jnp.where(entry_block[:, None] == names[None, :], block_home[None, :], 0), axis=1
    )
    slot_ids = jnp.arange(slots, dtype=jnp.int32)
    live = slot_ids < entry_count[0]
    holder = jnp.where(live, stored // blocks_here, -1)
    earlier = (holder[:, None] == holder[None, :]) & (slot_ids[None, :] < slot_ids[:, None])
    places = jnp.sum(earlier.astype(jnp.int32), axis=1)
    code = stored % blocks_here * (width // BLK_R) + entry_row
    target = jnp.where(live, holder * capacity + places, -1)
    room_ids = jnp.arange(holders * capacity, dtype=jnp.int32)
    wanted = (
        jnp.sum(jnp.where(target[None, :] == room_ids[:, None], code[None, :] + 1, 0), axis=1) - 1
    )
    wanted = wanted.reshape(holders, 1, capacity).astype(f32)

    angle_rows = jnp.stack(
        angle_pieces(row_angle.astype(f32)) + [row_weight.astype(f32)], axis=0
    )
    send = jnp.concatenate(
        [
            jnp.broadcast_to(angle_rows[None], (holders, PIECES - 1, width)),
            jnp.pad(wanted, ((0, 0), (0, 0), (0, width - capacity))),
        ],
        axis=1,
    ).astype(bf16)
    left = lax.all_to_all(send, "rows", split_axis=0, concat_axis=0, tiled=True)
    codes = left[:, PIECES - 1, :capacity].astype(jnp.int32).reshape(holders * capacity)

    freq = wear_freq.reshape(blocks_here, 1, BLK_P)
    scale = (param_scale.astype(f32) * (1.0 / math.sqrt(8.0 * BLK_P))).astype(bf16)
    scale = scale.reshape(blocks_here, 1, BLK_P)
    kind = lax.broadcasted_iota(jnp.int32, (1, PIECES, 1), 1)
    right = jnp.concatenate(
        [
            jnp.where(kind < PIECES - 2, freq, jnp.zeros_like(freq)),
            jnp.where(kind == PIECES - 2, scale, jnp.zeros_like(scale)),
        ],
        axis=2,
    )
    me = lax.axis_index("rows")
    core = lax.axis_index("grp") % 2
    side, position = me % 2, me // 2
    ring = holders // 2

    jac = None
    waiting = []
    arrived = []
    for k in range(ring):
        where = jnp.stack([(position + 2 * ring - 1 - k) % ring, side])
        near, far, jac = forward(codes, where, left, right, vectors, capacity, jac)
        waiting.append((near, swap(far, "rows", 1)))
        if k > 0:
            before, got = waiting[k - 1]
            pair = before + got
            if k == ring - 1:
                pair = pair.astype(bf16)
            older = arrived[: ring - 3]
            codes, pair, older = lax.optimization_barrier((codes, pair, older))
            arrived = older + arrived[ring - 3 :]
            arrived.append(shift(pair, "rows", -k))
    near, got = waiting[-1]
    got, early = lax.optimization_barrier((got, arrived[:-1]))
    arrived = early + arrived[-1:]
    outputs = near + got
    for pair in arrived:
        outputs = outputs + pair.astype(f32)
    outputs = outputs.astype(bf16)

    same = [outputs] + [shift(outputs, "rows", k) for k in range(1, ring)]
    pieces = same + [swap(piece, "rows", 1) for piece in same]

    def terms(first, pieces):
        where = jnp.stack([position, side, first])
        return backward(codes, where, jac, pieces, quarter, capacity)

    quarter = blocks_here // 4
    pairs = []
    sums = []
    for chunk in range(2):
        given, pieces = terms((2 * (1 - core) + chunk) * quarter, pieces)
        given = swap(given, "grp", 1)
        kept, pieces = terms((2 * core + chunk) * quarter, pieces)
        chunk_sum = kept + given
        bit = 2
        pair = (chunk_sum, jnp.zeros_like(chunk_sum))
        while bit < members:
            rounded = lax.reduce_precision(chunk_sum, 8, 7)
            sent = rounded.astype(bf16)
            codes, sent, sums = lax.optimization_barrier((codes, sent, sums))
            pair = (sent, swap(sent, "grp", bit))
            chunk_sum = rounded + pair[1].astype(f32)
            bit *= 2
        sums.append(chunk_sum)
        pairs.append(pair)
    where = core.reshape(1)
    early = place(where, None, ((True, 0), (False, 0)), ((sums[0],), (swap(sums[0], "grp", 1),)))
    last = pairs[1]
    across = tuple(swap(array, "grp", 1) for array in last)
    return place(where, early, ((True, 1), (False, 1)), (last, across))


def solution(mesh):
    return jax.shard_map(
        body,
        mesh=mesh,
        in_specs=(
            P(None, "rows"),
            P("rows"),
            P("rows"),
            P(("rows", "grp")),
            P(("rows", "grp")),
            P(("rows", "grp")),
            P(("rows", "grp")),
            P(("rows", "grp")),
            P(),
        ),
        out_specs=P(None, "rows"),
        check_vma=False,
    )
```

```python
import functools
import math

import jax
import jax.numpy as jnp
from jax import lax
from jax.experimental import pallas as pl
from jax.experimental.pallas import tpu as pltpu
from jax.sharding import PartitionSpec as P

BLK_R = 256
BLK_P = 512
PIECES = 8
RING = 8

f32 = jnp.float32
bf16 = jnp.bfloat16

COS_POLY = (
    1.4142134965678816,
    -6.978850988354285,
    5.7394611717976565,
    -1.8835629903409246,
    0.3106981920279389,
)


def turn_constants():
    constants = []
    rest = 1.0 / (2.0 * math.pi)
    for _ in range(3):
        mantissa, exponent = math.frexp(rest)
        constant = math.ldexp(round(mantissa * 256.0) / 256.0, exponent)
        constants.append(constant)
        rest -= constant
    return constants


def angle_pieces(angles):
    out = []
    for constant in turn_constants():
        exact = angles * constant
        top = lax.reduce_precision(exact, 8, 7)
        out += [top, exact - top]
    return out


def collect(codes, todo, start, places, low, high):
    def visit(step, found):
        todo[found] = start + step
        code = codes[start + step]
        return found + ((code >= low) & (code < high)).astype(jnp.int32)

    return lax.fori_loop(0, places, visit, 0, unroll=8 if places % 8 == 0 else 1)


def entry_cost(entries, vector_count):
    return pl.CostEstimate(flops=entries, bytes_accessed=vector_count, transcendentals=0)


def forward_kernel(blocks, capacity, codes, where, left, right, vectors, *refs):
    near, far, jac, todo, columns, part, even, odd, sems = refs[-9:]
    spare = codes.shape[0]
    rows = left.shape[2] // BLK_R
    part[...] = jnp.zeros_like(part)
    start = 2 * capacity * where[0]
    found = collect(codes, todo, start, 2 * capacity, 0, blocks * rows)
    for k in range(2):
        for at in range(0, left.shape[2], 128):
            lanes = left[2 * where[0] + k, :, at : at + 128]
            columns[k, at : at + 128, :] = lanes.astype(f32).T.astype(bf16)
    steps = (found + 1) // 2

    def decode(place):
        code = codes[place]
        group = lax.div(place, capacity)
        away = jnp.where(lax.rem(group, 2) == where[1], 0, 1)
        return lax.div(code, rows), lax.rem(code, rows), group, away

    def make(buffer, place):
        block, row, group, _ = decode(place)
        at = pl.ds(pl.multiple_of(row * BLK_R, BLK_R), BLK_R)
        both = jnp.dot(
            columns[lax.rem(group, 2), at, :], right[block], preferred_element_type=f32
        )
        turns, weight = both[:, :BLK_P], both[:, BLK_P:]
        rest = turns - jnp.round(turns)
        square = rest * rest
        root = COS_POLY[4] * square + COS_POLY[3]
        for k in (2, 1, 0):
            root = root * square + COS_POLY[k]
        buffer[...] = (weight * (root * root - 1.0)).astype(bf16)

    def apply(buffer, place, keep):
        block, row, _, away = decode(place)
        chosen = vectors[:, pl.ds(pl.multiple_of(block * BLK_P, BLK_P), BLK_P)]
        term = lax.dot_general(
            buffer[...], chosen, (((1,), (1,)), ((), ())), preferred_element_type=f32
        )
        if keep is not None:
            term = jnp.where(keep, term, 0.0)
        part[away, :, pl.ds(pl.multiple_of(row * BLK_R, BLK_R), BLK_R)] += term.T

    def save(buffer, parity, which, place):
        return pltpu.make_async_copy(buffer.at[parity], jac.at[place], sems.at[parity, which])

    def step(turn, before):
        parity = lax.rem(turn, 2)
        first = todo[2 * turn]
        paired = 2 * turn + 1 < found
        second = todo[jnp.where(paired, 2 * turn + 1, 2 * turn)]

        @pl.when(turn >= 2)
        def _():
            save(even, parity, 0, 0).wait()
            save(odd, parity, 1, 0).wait()

        apply(odd.at[1 - parity], before, turn > 0)
        make(even.at[parity], first)
        save(even, parity, 0, first).start()
        apply(even.at[parity], first, None)
        make(odd.at[parity], second)
        save(odd, parity, 1, jnp.where(paired, second, spare)).start()
        return second

    last = lax.fori_loop(0, steps, step, todo[0])

    @pl.when((found > 0) & (lax.rem(found, 2) == 0))
    def _():
        apply(odd.at[lax.rem(steps + 1, 2)], last, None)

    for back in (1, 2):
        @pl.when(steps >= back)
        def _():
            parity = lax.rem(steps + back, 2)
            save(even, parity, 0, 0).wait()
            save(odd, parity, 1, 0).wait()

    near[...] = part[0]
    far[...] = part[1]


def forward(codes, where, left, right, vectors, capacity, jac):
    _, _, width = left.shape
    blocks = right.shape[0]
    room = codes.shape[0]
    count = vectors.shape[0]
    vmem = pl.BlockSpec(memory_space=pltpu.VMEM)
    smem = pl.BlockSpec(memory_space=pltpu.SMEM)
    hbm = pl.BlockSpec(memory_space=pltpu.HBM)
    held = [] if jac is None else [jac]
    return pl.pallas_call(
        functools.partial(forward_kernel, blocks, capacity),
        out_shape=(jax.ShapeDtypeStruct((count, width), f32),) * 2
        + (pltpu.HBM((room + 1, BLK_R, BLK_P), bf16),),
        in_specs=[smem, smem, vmem, vmem, vmem] + [hbm] * len(held),
        out_specs=(vmem, vmem, hbm),
        scratch_shapes=[
            pltpu.SMEM((2 * capacity + 1,), jnp.int32),
            pltpu.VMEM((2, width, PIECES), bf16),
            pltpu.VMEM((2, count, width), f32),
            pltpu.VMEM((2, BLK_R, BLK_P), bf16),
            pltpu.VMEM((2, BLK_R, BLK_P), bf16),
            pltpu.SemaphoreType.DMA((2, 2)),
        ],
        input_output_aliases={5: 2} if held else {},
        compiler_params=pltpu.CompilerParams(vmem_limit_bytes=16 << 20),
        cost_estimate=entry_cost(2 * capacity, count),
        name="forward",
    )(codes, where, left, right, vectors, *held)


def backward_kernel(capacity, ring, codes, where, jac, *refs):
    *pieces, out, gathered, todo, buffers, sems = refs
    here = out.shape[1] // BLK_P
    depth = buffers.shape[0]

    rows = gathered.shape[2] // BLK_R
    found = collect(codes, todo, 0, codes.shape[0], where[2] * rows, (where[2] + here) * rows)

    def load(turn):
        slot = lax.rem(turn, depth)
        return pltpu.make_async_copy(jac.at[todo[turn]], buffers.at[slot], sems.at[slot])

    def prime(turn, carry):
        load(turn).start()
        return carry

    lax.fori_loop(0, jnp.minimum(found, depth - 1), prime, 0)
    for k in range(len(pieces)):
        gathered[k] = pieces[k][...]
    out[...] = jnp.zeros_like(out)

    def step(turn, carry):
        @pl.when(turn + depth - 1 < found)
        def _():
            load(turn + depth - 1).start()

        place = todo[turn]
        code = codes[place]
        block, row = lax.div(code, rows) - where[2], lax.rem(code, rows)
        behind = lax.rem(where[0] - lax.div(place, 2 * capacity) + ring, ring)
        near = lax.rem(lax.div(place, capacity), 2) == where[1]
        piece = jnp.where(near, behind, ring + behind)
        chosen = gathered[piece, :, pl.ds(pl.multiple_of(row * BLK_R, BLK_R), BLK_R)]
        at = pl.ds(pl.multiple_of(block * BLK_P, BLK_P), BLK_P)
        slot = lax.rem(turn, depth)
        load(turn).wait()
        out[:, at] += jnp.dot(chosen, buffers[slot], preferred_element_type=f32)
        return carry

    lax.fori_loop(0, found, step, 0)


def joined_backward_kernel(capacity, ring, *refs):
    *inputs, gathered, out, todo, buffers, sems = refs
    backward_kernel(capacity, ring, *inputs, out, gathered, todo, buffers, sems)


def backward(codes, where, jac, pieces, here, capacity):
    joined = not isinstance(pieces, list)
    smem = pl.BlockSpec(memory_space=pltpu.SMEM)
    vmem = pl.BlockSpec(memory_space=pltpu.VMEM)
    hbm = pl.BlockSpec(memory_space=pl.ANY)
    sources = [pieces] if joined else pieces
    count, width = sources[0].shape[-2:]
    total = pieces.shape[0] if joined else len(pieces)
    terms = jax.ShapeDtypeStruct((count, here * BLK_P), f32)
    gathered = jax.ShapeDtypeStruct((total, count, width), bf16)
    kernel = joined_backward_kernel if joined else backward_kernel
    result = pl.pallas_call(
        functools.partial(kernel, capacity, total // 2),
        out_shape=terms if joined else (terms, gathered),
        in_specs=[smem, smem, hbm] + [vmem] * len(sources),
        out_specs=vmem if joined else (vmem, vmem),
        scratch_shapes=[
            pltpu.SMEM((codes.shape[0] + 1,), jnp.int32),
            pltpu.VMEM((RING, BLK_R, BLK_P), bf16),
            pltpu.SemaphoreType.DMA((RING,)),
        ],
        compiler_params=pltpu.CompilerParams(vmem_limit_bytes=36 << 20),
        cost_estimate=entry_cost(codes.shape[0] // 8, count),
        name="backward",
    )(codes, where, jac, *sources)
    return (result, pieces) if joined else result


def place_kernel(quarters, addends, where, *refs):
    *sources, out, sums, sems = refs
    sources = sources[-addends * len(quarters) :]
    wide = sums.shape[2]
    copies = []
    for k, (mine, chunk) in enumerate(quarters):
        total = sources[addends * k][...].astype(f32)
        for source in sources[addends * k + 1 : addends * (k + 1)]:
            total = total + source[...].astype(f32)
        sums[k] = total
        half = where[0] if mine else 1 - where[0]
        at = pl.ds(pl.multiple_of((2 * half + chunk) * wide, wide), wide)
        copies.append(pltpu.make_async_copy(sums.at[k], out.at[:, at], sems.at[k]))
        copies[-1].start()
    for copy in copies:
        copy.wait()


def place(where, into, quarters, groups):
    hbm = pl.BlockSpec(memory_space=pl.ANY)
    vmem = pl.BlockSpec(memory_space=pltpu.VMEM)
    sources = [array for group in groups for array in group]
    count, wide = sources[0].shape
    held = [] if into is None else [into]
    return pl.pallas_call(
        functools.partial(place_kernel, quarters, len(groups[0])),
        out_shape=jax.ShapeDtypeStruct((count, 4 * wide), f32),
        in_specs=[pl.BlockSpec(memory_space=pltpu.SMEM)] + [hbm] * len(held) + [vmem] * len(sources),
        out_specs=hbm,
        scratch_shapes=[
            pltpu.VMEM((len(quarters), count, wide), f32),
            pltpu.SemaphoreType.DMA((len(quarters),)),
        ],
        input_output_aliases={1: 0} if held else {},
        compiler_params=pltpu.CompilerParams(vmem_limit_bytes=10 << 20),
        name="place",
    )(where, *held, *sources)


def swap(array, axis, bit):
    return lax.ppermute(array, axis, [(i, i ^ bit) for i in range(lax.axis_size(axis))])


def shift(array, axis, steps):
    size = lax.axis_size(axis)
    return lax.ppermute(array, axis, [(i, (i + 2 * steps) % size) for i in range(size)])


def body(
    vectors,
    wear_freq,
    param_scale,
    row_angle,
    row_weight,
    entry_block,
    entry_row,
    entry_count,
    block_home,
):
    holders = lax.axis_size("rows")
    members = lax.axis_size("grp")
    vector_count = vectors.shape[0]
    blocks_here = vectors.shape[1] // BLK_P
    slots = entry_block.shape[0]
    capacity = slots // holders
    width = row_angle.shape[0]

    names = jnp.arange(block_home.shape[0], dtype=jnp.int32)
    stored = jnp.sum(
        jnp.where(entry_block[:, None] == names[None, :], block_home[None, :], 0), axis=1
    )
    slot_ids = jnp.arange(slots, dtype=jnp.int32)
    live = slot_ids < entry_count[0]
    holder = jnp.where(live, stored // blocks_here, -1)
    earlier = (holder[:, None] == holder[None, :]) & (slot_ids[None, :] < slot_ids[:, None])
    places = jnp.sum(earlier.astype(jnp.int32), axis=1)
    code = stored % blocks_here * (width // BLK_R) + entry_row
    target = jnp.where(live, holder * capacity + places, -1)
    room_ids = jnp.arange(holders * capacity, dtype=jnp.int32)
    wanted = (
        jnp.sum(jnp.where(target[None, :] == room_ids[:, None], code[None, :] + 1, 0), axis=1) - 1
    )
    wanted = wanted.reshape(holders, 1, capacity).astype(f32)

    kind = lax.broadcasted_iota(jnp.int32, (1, PIECES, 1), 1)
    send = jnp.pad(wanted, ((0, 0), (0, 0), (0, width - capacity)))
    for k, piece in enumerate(angle_pieces(row_angle.astype(f32)) + [row_weight.astype(f32)]):
        send = jnp.where(kind == k, piece[None, None, :], send)
    send = send.astype(bf16)
    left = lax.all_to_all(send, "rows", split_axis=0, concat_axis=0, tiled=True)
    codes = left[:, PIECES - 1, :capacity].astype(jnp.int32).reshape(holders * capacity)

    freq = wear_freq.reshape(blocks_here, 1, BLK_P)
    scale = (param_scale.astype(f32) * (1.0 / math.sqrt(8.0 * BLK_P))).astype(bf16)
    scale = scale.reshape(blocks_here, 1, BLK_P)
    right = jnp.concatenate(
        [
            jnp.where(kind < PIECES - 2, freq, jnp.zeros_like(freq)),
            jnp.where(kind == PIECES - 2, scale, jnp.zeros_like(scale)),
        ],
        axis=2,
    )
    me = lax.axis_index("rows")
    core = lax.axis_index("grp") % 2
    side, position = me % 2, me // 2
    ring = holders // 2

    jac = None
    waiting = []
    arrived = []
    for k in range(ring):
        where = jnp.stack([(position + 2 * ring - 1 - k) % ring, side])
        near, far, jac = forward(codes, where, left, right, vectors, capacity, jac)
        waiting.append((near, swap(far, "rows", 1)))
        if k > 0:
            before, got = waiting[k - 1]
            pair = before + got
            if k == ring - 1:
                pair = pair.astype(bf16)
            older = arrived[: ring - 3]
            codes, pair, older = lax.optimization_barrier((codes, pair, older))
            arrived = older + arrived[ring - 3 :]
            arrived.append(shift(pair, "rows", -k))
    near, got = waiting[-1]
    got, early = lax.optimization_barrier((got, arrived[:-1]))
    arrived = early + arrived[-1:]
    outputs = near + got
    for pair in arrived:
        outputs = outputs + pair.astype(f32)
    outputs = outputs.astype(bf16)

    same = [outputs] + [shift(outputs, "rows", k) for k in range(1, ring)]
    pieces = same + [swap(piece, "rows", 1) for piece in same]

    def terms(first, pieces):
        where = jnp.stack([position, side, first])
        return backward(codes, where, jac, pieces, quarter, capacity)

    quarter = blocks_here // 4
    pairs = []
    sums = []
    for chunk in range(2):
        given, pieces = terms((2 * (1 - core) + chunk) * quarter, pieces)
        given = swap(given, "grp", 1)
        kept, pieces = terms((2 * core + chunk) * quarter, pieces)
        chunk_sum = kept + given
        bit = 2
        pair = (chunk_sum, jnp.zeros_like(chunk_sum))
        while bit < members:
            rounded = lax.reduce_precision(chunk_sum, 8, 7)
            sent = rounded.astype(bf16)
            codes, sent, sums = lax.optimization_barrier((codes, sent, sums))
            pair = (sent, swap(sent, "grp", bit))
            chunk_sum = rounded + pair[1].astype(f32)
            bit *= 2
        sums.append(chunk_sum)
        pairs.append(pair)
    where = core.reshape(1)
    early = place(where, None, ((True, 0), (False, 0)), ((sums[0],), (swap(sums[0], "grp", 1),)))
    last = pairs[1]
    across = tuple(swap(array, "grp", 1) for array in last)
    return place(where, early, ((True, 1), (False, 1)), (last, across))


def solution(mesh):
    return jax.shard_map(
        body,
        mesh=mesh,
        in_specs=(
            P(None, "rows"),
            P("rows"),
            P("rows"),
            P(("rows", "grp")),
            P(("rows", "grp")),
            P(("rows", "grp")),
            P(("rows", "grp")),
            P(("rows", "grp")),
            P(),
        ),
        out_specs=P(None, "rows"),
        check_vma=False,
    )
```

```python
import functools
import math

import jax
import jax.numpy as jnp
from jax import lax
from jax.experimental import pallas as pl
from jax.experimental.pallas import tpu as pltpu
from jax.sharding import PartitionSpec as P

BLK_R = 256
BLK_P = 512
PIECES = 8
RING = 8

f32 = jnp.float32
bf16 = jnp.bfloat16

COS_POLY = (
    1.4142134965678816,
    -6.978850988354285,
    5.7394611717976565,
    -1.8835629903409246,
    0.3106981920279389,
)


def turn_constants():
    constants = []
    rest = 1.0 / (2.0 * math.pi)
    for _ in range(3):
        mantissa, exponent = math.frexp(rest)
        constant = math.ldexp(round(mantissa * 256.0) / 256.0, exponent)
        constants.append(constant)
        rest -= constant
    return constants


def angle_pieces(angles):
    out = []
    for constant in turn_constants():
        exact = angles * constant
        top = lax.reduce_precision(exact, 8, 7)
        out += [top, exact - top]
    return out


def collect(codes, todo, start, places, low, high):
    def visit(step, found):
        todo[found] = start + step
        code = codes[start + step]
        return found + ((code >= low) & (code < high)).astype(jnp.int32)

    return lax.fori_loop(0, places, visit, 0, unroll=8 if places % 8 == 0 else 1)


def entry_cost(entries, vector_count):
    return pl.CostEstimate(flops=entries, bytes_accessed=vector_count, transcendentals=0)


def forward_kernel(blocks, capacity, codes, where, left, right, vectors, *refs):
    near, far, jac, todo, columns, part, even, odd, sems = refs[-9:]
    spare = codes.shape[0]
    rows = left.shape[2] // BLK_R
    part[...] = jnp.zeros_like(part)
    start = 2 * capacity * where[0]
    found = collect(codes, todo, start, 2 * capacity, 0, blocks * rows)
    for k in range(2):
        for at in range(0, left.shape[2], 128):
            lanes = left[2 * where[0] + k, :, at : at + 128]
            columns[k, at : at + 128, :] = lanes.astype(f32).T.astype(bf16)
    steps = (found + 1) // 2

    def decode(place):
        code = codes[place]
        group = lax.div(place, capacity)
        away = jnp.where(lax.rem(group, 2) == where[1], 0, 1)
        return lax.div(code, rows), lax.rem(code, rows), group, away

    def make(buffer, place):
        block, row, group, _ = decode(place)
        at = pl.ds(pl.multiple_of(row * BLK_R, BLK_R), BLK_R)
        both = jnp.dot(
            columns[lax.rem(group, 2), at, :], right[block], preferred_element_type=f32
        )
        turns, weight = both[:, :BLK_P], both[:, BLK_P:]
        rest = turns - jnp.round(turns)
        square = rest * rest
        root = COS_POLY[4] * square + COS_POLY[3]
        for k in (2, 1, 0):
            root = root * square + COS_POLY[k]
        buffer[...] = (weight * (root * root - 1.0)).astype(bf16)

    def apply(buffer, place, keep):
        block, row, _, away = decode(place)
        chosen = vectors[:, pl.ds(pl.multiple_of(block * BLK_P, BLK_P), BLK_P)]
        term = lax.dot_general(
            chosen, buffer[...], (((1,), (1,)), ((), ())), preferred_element_type=f32
        )
        if keep is not None:
            term = jnp.where(keep, term, 0.0)
        part[away, :, pl.ds(pl.multiple_of(row * BLK_R, BLK_R), BLK_R)] += term

    def save(buffer, parity, which, place):
        return pltpu.make_async_copy(buffer.at[parity], jac.at[place], sems.at[parity, which])

    def step(turn, before):
        parity = lax.rem(turn, 2)
        first = todo[2 * turn]
        paired = 2 * turn + 1 < found
        second = todo[jnp.where(paired, 2 * turn + 1, 2 * turn)]

        @pl.when(turn >= 2)
        def _():
            save(even, parity, 0, 0).wait()
            save(odd, parity, 1, 0).wait()

        apply(odd.at[1 - parity], before, turn > 0)
        make(even.at[parity], first)
        save(even, parity, 0, first).start()
        apply(even.at[parity], first, None)
        make(odd.at[parity], second)
        save(odd, parity, 1, jnp.where(paired, second, spare)).start()
        return second

    last = lax.fori_loop(0, steps, step, todo[0])

    @pl.when((found > 0) & (lax.rem(found, 2) == 0))
    def _():
        apply(odd.at[lax.rem(steps + 1, 2)], last, None)

    for back in (1, 2):
        @pl.when(steps >= back)
        def _():
            parity = lax.rem(steps + back, 2)
            save(even, parity, 0, 0).wait()
            save(odd, parity, 1, 0).wait()

    near[...] = part[0]
    far[...] = part[1]


def forward(codes, where, left, right, vectors, capacity, jac):
    _, _, width = left.shape
    blocks = right.shape[0]
    room = codes.shape[0]
    count = vectors.shape[0]
    vmem = pl.BlockSpec(memory_space=pltpu.VMEM)
    smem = pl.BlockSpec(memory_space=pltpu.SMEM)
    hbm = pl.BlockSpec(memory_space=pltpu.HBM)
    held = [] if jac is None else [jac]
    return pl.pallas_call(
        functools.partial(forward_kernel, blocks, capacity),
        out_shape=(jax.ShapeDtypeStruct((count, width), f32),) * 2
        + (pltpu.HBM((room + 1, BLK_R, BLK_P), bf16),),
        in_specs=[smem, smem, vmem, vmem, vmem] + [hbm] * len(held),
        out_specs=(vmem, vmem, hbm),
        scratch_shapes=[
            pltpu.SMEM((2 * capacity + 1,), jnp.int32),
            pltpu.VMEM((2, width, PIECES), bf16),
            pltpu.VMEM((2, count, width), f32),
            pltpu.VMEM((2, BLK_R, BLK_P), bf16),
            pltpu.VMEM((2, BLK_R, BLK_P), bf16),
            pltpu.SemaphoreType.DMA((2, 2)),
        ],
        input_output_aliases={5: 2} if held else {},
        compiler_params=pltpu.CompilerParams(vmem_limit_bytes=16 << 20),
        cost_estimate=entry_cost(2 * capacity, count),
        name="forward",
    )(codes, where, left, right, vectors, *held)


def backward_kernel(capacity, ring, codes, where, jac, *refs):
    *pieces, out, gathered, todo, buffers, sems = refs
    here = out.shape[1] // BLK_P
    depth = buffers.shape[0]

    rows = gathered.shape[2] // BLK_R
    found = collect(codes, todo, 0, codes.shape[0], where[2] * rows, (where[2] + here) * rows)

    def load(turn):
        slot = lax.rem(turn, depth)
        return pltpu.make_async_copy(jac.at[todo[turn]], buffers.at[slot], sems.at[slot])

    def prime(turn, carry):
        load(turn).start()
        return carry

    lax.fori_loop(0, jnp.minimum(found, depth - 1), prime, 0)
    for k in range(len(pieces)):
        gathered[k] = pieces[k][...]
    out[...] = jnp.zeros_like(out)

    def step(turn, carry):
        @pl.when(turn + depth - 1 < found)
        def _():
            load(turn + depth - 1).start()

        place = todo[turn]
        code = codes[place]
        block, row = lax.div(code, rows) - where[2], lax.rem(code, rows)
        behind = lax.rem(where[0] - lax.div(place, 2 * capacity) + ring, ring)
        near = lax.rem(lax.div(place, capacity), 2) == where[1]
        piece = jnp.where(near, behind, ring + behind)
        chosen = gathered[piece, :, pl.ds(pl.multiple_of(row * BLK_R, BLK_R), BLK_R)]
        at = pl.ds(pl.multiple_of(block * BLK_P, BLK_P), BLK_P)
        slot = lax.rem(turn, depth)
        load(turn).wait()
        out[:, at] += jnp.dot(chosen, buffers[slot], preferred_element_type=f32)
        return carry

    lax.fori_loop(0, found, step, 0)


def joined_backward_kernel(capacity, ring, *refs):
    *inputs, gathered, out, todo, buffers, sems = refs
    backward_kernel(capacity, ring, *inputs, out, gathered, todo, buffers, sems)


def backward(codes, where, jac, pieces, here, capacity):
    joined = not isinstance(pieces, list)
    smem = pl.BlockSpec(memory_space=pltpu.SMEM)
    vmem = pl.BlockSpec(memory_space=pltpu.VMEM)
    hbm = pl.BlockSpec(memory_space=pl.ANY)
    sources = [pieces] if joined else pieces
    count, width = sources[0].shape[-2:]
    total = pieces.shape[0] if joined else len(pieces)
    terms = jax.ShapeDtypeStruct((count, here * BLK_P), f32)
    gathered = jax.ShapeDtypeStruct((total, count, width), bf16)
    kernel = joined_backward_kernel if joined else backward_kernel
    result = pl.pallas_call(
        functools.partial(kernel, capacity, total // 2),
        out_shape=terms if joined else (terms, gathered),
        in_specs=[smem, smem, hbm] + [vmem] * len(sources),
        out_specs=vmem if joined else (vmem, vmem),
        scratch_shapes=[
            pltpu.SMEM((codes.shape[0] + 1,), jnp.int32),
            pltpu.VMEM((RING, BLK_R, BLK_P), bf16),
            pltpu.SemaphoreType.DMA((RING,)),
        ],
        compiler_params=pltpu.CompilerParams(vmem_limit_bytes=36 << 20),
        cost_estimate=entry_cost(codes.shape[0] // 8, count),
        name="backward",
    )(codes, where, jac, *sources)
    return (result, pieces) if joined else result


def place_kernel(quarters, addends, where, *refs):
    *sources, out, sums, sems = refs
    sources = sources[-addends * len(quarters) :]
    wide = sums.shape[2]
    copies = []
    for k, (mine, chunk) in enumerate(quarters):
        total = sources[addends * k][...].astype(f32)
        for source in sources[addends * k + 1 : addends * (k + 1)]:
            total = total + source[...].astype(f32)
        sums[k] = total
        half = where[0] if mine else 1 - where[0]
        at = pl.ds(pl.multiple_of((2 * half + chunk) * wide, wide), wide)
        copies.append(pltpu.make_async_copy(sums.at[k], out.at[:, at], sems.at[k]))
        copies[-1].start()
    for copy in copies:
        copy.wait()


def place(where, into, quarters, groups):
    hbm = pl.BlockSpec(memory_space=pl.ANY)
    vmem = pl.BlockSpec(memory_space=pltpu.VMEM)
    sources = [array for group in groups for array in group]
    count, wide = sources[0].shape
    held = [] if into is None else [into]
    return pl.pallas_call(
        functools.partial(place_kernel, quarters, len(groups[0])),
        out_shape=jax.ShapeDtypeStruct((count, 4 * wide), f32),
        in_specs=[pl.BlockSpec(memory_space=pltpu.SMEM)] + [hbm] * len(held) + [vmem] * len(sources),
        out_specs=hbm,
        scratch_shapes=[
            pltpu.VMEM((len(quarters), count, wide), f32),
            pltpu.SemaphoreType.DMA((len(quarters),)),
        ],
        input_output_aliases={1: 0} if held else {},
        compiler_params=pltpu.CompilerParams(vmem_limit_bytes=10 << 20),
        name="place",
    )(where, *held, *sources)


def swap(array, axis, bit):
    return lax.ppermute(array, axis, [(i, i ^ bit) for i in range(lax.axis_size(axis))])


def shift(array, axis, steps):
    size = lax.axis_size(axis)
    return lax.ppermute(array, axis, [(i, (i + 2 * steps) % size) for i in range(size)])


def body(
    vectors,
    wear_freq,
    param_scale,
    row_angle,
    row_weight,
    entry_block,
    entry_row,
    entry_count,
    block_home,
):
    holders = lax.axis_size("rows")
    members = lax.axis_size("grp")
    vector_count = vectors.shape[0]
    blocks_here = vectors.shape[1] // BLK_P
    slots = entry_block.shape[0]
    capacity = slots // holders
    width = row_angle.shape[0]

    names = jnp.arange(block_home.shape[0], dtype=jnp.int32)
    stored = jnp.sum(
        jnp.where(entry_block[:, None] == names[None, :], block_home[None, :], 0), axis=1
    )
    slot_ids = jnp.arange(slots, dtype=jnp.int32)
    live = slot_ids < entry_count[0]
    holder = jnp.where(live, stored // blocks_here, -1)
    earlier = (holder[:, None] == holder[None, :]) & (slot_ids[None, :] < slot_ids[:, None])
    places = jnp.sum(earlier.astype(jnp.int32), axis=1)
    code = stored % blocks_here * (width // BLK_R) + entry_row
    target = jnp.where(live, holder * capacity + places, -1)
    room_ids = jnp.arange(holders * capacity, dtype=jnp.int32)
    wanted = (
        jnp.sum(jnp.where(target[None, :] == room_ids[:, None], code[None, :] + 1, 0), axis=1) - 1
    )
    wanted = wanted.reshape(holders, 1, capacity).astype(f32)

    angle_rows = jnp.stack(
        angle_pieces(row_angle.astype(f32)) + [row_weight.astype(f32)], axis=0
    )
    send = jnp.concatenate(
        [
            jnp.broadcast_to(angle_rows[None], (holders, PIECES - 1, width)),
            jnp.pad(wanted, ((0, 0), (0, 0), (0, width - capacity))),
        ],
        axis=1,
    ).astype(bf16)
    left = lax.all_to_all(send, "rows", split_axis=0, concat_axis=0, tiled=True)
    codes = left[:, PIECES - 1, :capacity].astype(jnp.int32).reshape(holders * capacity)

    freq = wear_freq.reshape(blocks_here, 1, BLK_P)
    scale = (param_scale.astype(f32) * (1.0 / math.sqrt(8.0 * BLK_P))).astype(bf16)
    scale = scale.reshape(blocks_here, 1, BLK_P)
    kind = lax.broadcasted_iota(jnp.int32, (1, PIECES, 1), 1)
    right = jnp.concatenate(
        [
            jnp.where(kind < PIECES - 2, freq, jnp.zeros_like(freq)),
            jnp.where(kind == PIECES - 2, scale, jnp.zeros_like(scale)),
        ],
        axis=2,
    )
    me = lax.axis_index("rows")
    core = lax.axis_index("grp") % 2
    side, position = me % 2, me // 2
    ring = holders // 2

    jac = None
    waiting = []
    arrived = []
    for k in range(ring):
        where = jnp.stack([(position + 2 * ring - 1 - k) % ring, side])
        near, far, jac = forward(codes, where, left, right, vectors, capacity, jac)
        waiting.append((near, swap(far, "rows", 1)))
        if k > 0:
            before, got = waiting[k - 1]
            pair = before + got
            if k == ring - 1:
                pair = pair.astype(bf16)
            older = arrived[: ring - 3]
            codes, pair, older = lax.optimization_barrier((codes, pair, older))
            arrived = older + arrived[ring - 3 :]
            arrived.append(shift(pair, "rows", -k))
    near, got = waiting[-1]
    got, early = lax.optimization_barrier((got, arrived[:-1]))
    arrived = early + arrived[-1:]
    outputs = near + got
    for pair in arrived:
        outputs = outputs + pair.astype(f32)
    outputs = outputs.astype(bf16)

    same = [outputs] + [shift(outputs, "rows", k) for k in range(1, ring)]
    pieces = same + [swap(piece, "rows", 1) for piece in same]

    def terms(first, pieces):
        where = jnp.stack([position, side, first])
        return backward(codes, where, jac, pieces, quarter, capacity)

    quarter = blocks_here // 4
    pairs = []
    sums = []
    for chunk in range(2):
        given, pieces = terms((2 * (1 - core) + chunk) * quarter, pieces)
        given = swap(given, "grp", 1)
        kept, pieces = terms((2 * core + chunk) * quarter, pieces)
        chunk_sum = kept + given
        bit = 2
        pair = (chunk_sum, jnp.zeros_like(chunk_sum))
        while bit < members:
            rounded = lax.reduce_precision(chunk_sum, 8, 7)
            sent = rounded.astype(bf16)
            codes, sent, sums = lax.optimization_barrier((codes, sent, sums))
            pair = (sent, swap(sent, "grp", bit))
            chunk_sum = rounded + pair[1].astype(f32)
            bit *= 2
        sums.append(chunk_sum)
        pairs.append(pair)
    where = core.reshape(1)
    early = place(where, None, ((True, 0), (False, 0)), ((sums[0],), (swap(sums[0], "grp", 1),)))
    last = pairs[1]
    across = tuple(swap(array, "grp", 1) for array in last)
    return place(where, early, ((True, 1), (False, 1)), (last, across))


def solution(mesh):
    return jax.shard_map(
        body,
        mesh=mesh,
        in_specs=(
            P(None, "rows"),
            P("rows"),
            P("rows"),
            P(("rows", "grp")),
            P(("rows", "grp")),
            P(("rows", "grp")),
            P(("rows", "grp")),
            P(("rows", "grp")),
            P(),
        ),
        out_specs=P(None, "rows"),
        check_vma=False,
    )
```

```python
import functools
import math

import jax
import jax.numpy as jnp
from jax import lax
from jax.experimental import pallas as pl
from jax.experimental.pallas import tpu as pltpu
from jax.sharding import PartitionSpec as P

BLK_R = 256
BLK_P = 512
PIECES = 8
RING = 8

f32 = jnp.float32
bf16 = jnp.bfloat16

COS_POLY = (
    1.4142134965678816,
    -6.978850988354285,
    5.7394611717976565,
    -1.8835629903409246,
    0.3106981920279389,
)


def turn_constants():
    constants = []
    rest = 1.0 / (2.0 * math.pi)
    for _ in range(3):
        mantissa, exponent = math.frexp(rest)
        constant = math.ldexp(round(mantissa * 256.0) / 256.0, exponent)
        constants.append(constant)
        rest -= constant
    return constants


def angle_pieces(angles):
    out = []
    for constant in turn_constants():
        exact = angles * constant
        top = lax.reduce_precision(exact, 8, 7)
        out += [top, exact - top]
    return out


def collect(codes, todo, start, places, low, high):
    def visit(step, found):
        todo[found] = start + step
        code = codes[start + step]
        return found + ((code >= low) & (code < high)).astype(jnp.int32)

    return lax.fori_loop(0, places, visit, 0, unroll=8 if places % 8 == 0 else 1)


def entry_cost(entries, vector_count):
    return pl.CostEstimate(flops=entries, bytes_accessed=vector_count, transcendentals=0)


def forward_kernel(blocks, capacity, codes, where, left, right, vectors, *refs):
    near, far, jac, todo, columns, part, even, odd, sems = refs[-9:]
    spare = codes.shape[0]
    rows = left.shape[2] // BLK_R
    part[...] = jnp.zeros_like(part)
    start = 2 * capacity * where[0]
    found = collect(codes, todo, start, 2 * capacity, 0, blocks * rows)
    for k in range(2):
        for at in range(0, left.shape[2], 128):
            lanes = left[2 * where[0] + k, :, at : at + 128]
            columns[k, at : at + 128, :] = lanes.astype(f32).T.astype(bf16)
    steps = (found + 1) // 2

    def decode(place):
        code = codes[place]
        group = lax.div(place, capacity)
        away = jnp.where(lax.rem(group, 2) == where[1], 0, 1)
        return lax.div(code, rows), lax.rem(code, rows), group, away

    def make(buffer, place):
        block, row, group, _ = decode(place)
        at = pl.ds(pl.multiple_of(row * BLK_R, BLK_R), BLK_R)
        both = jnp.dot(
            columns[lax.rem(group, 2), at, :], right[block], preferred_element_type=f32
        )
        turns, weight = both[:, :BLK_P], both[:, BLK_P:]
        rest = turns - jnp.round(turns)
        square = rest * rest
        root = COS_POLY[4] * square + COS_POLY[3]
        for k in (2, 1, 0):
            root = root * square + COS_POLY[k]
        buffer[...] = (weight * (root * root - 1.0)).astype(bf16)

    def apply(buffer, place, keep):
        block, row, _, away = decode(place)
        chosen = vectors[:, pl.ds(pl.multiple_of(block * BLK_P, BLK_P), BLK_P)]
        term = lax.dot_general(
            chosen, buffer[...], (((1,), (1,)), ((), ())), preferred_element_type=f32
        )
        if keep is not None:
            term = jnp.where(keep, term, 0.0)
        part[away, :, pl.ds(pl.multiple_of(row * BLK_R, BLK_R), BLK_R)] += term

    def save(buffer, parity, which, place):
        return pltpu.make_async_copy(buffer.at[parity], jac.at[place], sems.at[parity, which])

    def step(turn, before):
        parity = lax.rem(turn, 2)
        first = todo[2 * turn]
        paired = 2 * turn + 1 < found
        second = todo[jnp.where(paired, 2 * turn + 1, 2 * turn)]

        @pl.when(turn >= 2)
        def _():
            save(even, parity, 0, 0).wait()
            save(odd, parity, 1, 0).wait()

        make(even.at[parity], first)
        save(even, parity, 0, first).start()
        apply(odd.at[1 - parity], before, turn > 0)
        make(odd.at[parity], second)
        save(odd, parity, 1, jnp.where(paired, second, spare)).start()
        apply(even.at[parity], first, None)
        return second

    last = lax.fori_loop(0, steps, step, todo[0])

    @pl.when((found > 0) & (lax.rem(found, 2) == 0))
    def _():
        apply(odd.at[lax.rem(steps + 1, 2)], last, None)

    for back in (1, 2):
        @pl.when(steps >= back)
        def _():
            parity = lax.rem(steps + back, 2)
            save(even, parity, 0, 0).wait()
            save(odd, parity, 1, 0).wait()

    near[...] = part[0]
    far[...] = part[1]


def forward(codes, where, left, right, vectors, capacity, jac):
    _, _, width = left.shape
    blocks = right.shape[0]
    room = codes.shape[0]
    count = vectors.shape[0]
    vmem = pl.BlockSpec(memory_space=pltpu.VMEM)
    smem = pl.BlockSpec(memory_space=pltpu.SMEM)
    hbm = pl.BlockSpec(memory_space=pltpu.HBM)
    held = [] if jac is None else [jac]
    return pl.pallas_call(
        functools.partial(forward_kernel, blocks, capacity),
        out_shape=(jax.ShapeDtypeStruct((count, width), f32),) * 2
        + (pltpu.HBM((room + 1, BLK_R, BLK_P), bf16),),
        in_specs=[smem, smem, vmem, vmem, vmem] + [hbm] * len(held),
        out_specs=(vmem, vmem, hbm),
        scratch_shapes=[
            pltpu.SMEM((2 * capacity + 1,), jnp.int32),
            pltpu.VMEM((2, width, PIECES), bf16),
            pltpu.VMEM((2, count, width), f32),
            pltpu.VMEM((2, BLK_R, BLK_P), bf16),
            pltpu.VMEM((2, BLK_R, BLK_P), bf16),
            pltpu.SemaphoreType.DMA((2, 2)),
        ],
        input_output_aliases={5: 2} if held else {},
        compiler_params=pltpu.CompilerParams(vmem_limit_bytes=16 << 20),
        cost_estimate=entry_cost(2 * capacity, count),
        name="forward",
    )(codes, where, left, right, vectors, *held)


def backward_kernel(capacity, ring, codes, where, jac, *refs):
    *pieces, out, gathered, todo, buffers, sems = refs
    here = out.shape[1] // BLK_P
    depth = buffers.shape[0]

    rows = gathered.shape[2] // BLK_R
    found = collect(codes, todo, 0, codes.shape[0], where[2] * rows, (where[2] + here) * rows)

    def load(turn):
        slot = lax.rem(turn, depth)
        return pltpu.make_async_copy(jac.at[todo[turn]], buffers.at[slot], sems.at[slot])

    def prime(turn, carry):
        load(turn).start()
        return carry

    lax.fori_loop(0, jnp.minimum(found, depth - 1), prime, 0)
    for k in range(len(pieces)):
        gathered[k] = pieces[k][...]
    out[...] = jnp.zeros_like(out)

    def step(turn, carry):
        @pl.when(turn + depth - 1 < found)
        def _():
            load(turn + depth - 1).start()

        place = todo[turn]
        code = codes[place]
        block, row = lax.div(code, rows) - where[2], lax.rem(code, rows)
        behind = lax.rem(where[0] - lax.div(place, 2 * capacity) + ring, ring)
        near = lax.rem(lax.div(place, capacity), 2) == where[1]
        piece = jnp.where(near, behind, ring + behind)
        chosen = gathered[piece, :, pl.ds(pl.multiple_of(row * BLK_R, BLK_R), BLK_R)]
        at = pl.ds(pl.multiple_of(block * BLK_P, BLK_P), BLK_P)
        slot = lax.rem(turn, depth)
        load(turn).wait()
        out[:, at] += jnp.dot(chosen, buffers[slot], preferred_element_type=f32)
        return carry

    lax.fori_loop(0, found, step, 0)


def joined_backward_kernel(capacity, ring, *refs):
    *inputs, gathered, out, todo, buffers, sems = refs
    backward_kernel(capacity, ring, *inputs, out, gathered, todo, buffers, sems)


def backward(codes, where, jac, pieces, here, capacity):
    joined = not isinstance(pieces, list)
    smem = pl.BlockSpec(memory_space=pltpu.SMEM)
    vmem = pl.BlockSpec(memory_space=pltpu.VMEM)
    hbm = pl.BlockSpec(memory_space=pl.ANY)
    sources = [pieces] if joined else pieces
    count, width = sources[0].shape[-2:]
    total = pieces.shape[0] if joined else len(pieces)
    terms = jax.ShapeDtypeStruct((count, here * BLK_P), f32)
    gathered = jax.ShapeDtypeStruct((total, count, width), bf16)
    kernel = joined_backward_kernel if joined else backward_kernel
    result = pl.pallas_call(
        functools.partial(kernel, capacity, total // 2),
        out_shape=terms if joined else (terms, gathered),
        in_specs=[smem, smem, hbm] + [vmem] * len(sources),
        out_specs=vmem if joined else (vmem, vmem),
        scratch_shapes=[
            pltpu.SMEM((codes.shape[0] + 1,), jnp.int32),
            pltpu.VMEM((RING, BLK_R, BLK_P), bf16),
            pltpu.SemaphoreType.DMA((RING,)),
        ],
        compiler_params=pltpu.CompilerParams(vmem_limit_bytes=36 << 20),
        cost_estimate=entry_cost(codes.shape[0] // 8, count),
        name="backward",
    )(codes, where, jac, *sources)
    return (result, pieces) if joined else result


def place_kernel(quarters, addends, where, *refs):
    *sources, out, sums, sems = refs
    sources = sources[-addends * len(quarters) :]
    wide = sums.shape[2]
    copies = []
    for k, (mine, chunk) in enumerate(quarters):
        total = sources[addends * k][...].astype(f32)
        for source in sources[addends * k + 1 : addends * (k + 1)]:
            total = total + source[...].astype(f32)
        sums[k] = total
        half = where[0] if mine else 1 - where[0]
        at = pl.ds(pl.multiple_of((2 * half + chunk) * wide, wide), wide)
        copies.append(pltpu.make_async_copy(sums.at[k], out.at[:, at], sems.at[k]))
        copies[-1].start()
    for copy in copies:
        copy.wait()


def place(where, into, quarters, groups):
    hbm = pl.BlockSpec(memory_space=pl.ANY)
    vmem = pl.BlockSpec(memory_space=pltpu.VMEM)
    sources = [array for group in groups for array in group]
    count, wide = sources[0].shape
    held = [] if into is None else [into]
    return pl.pallas_call(
        functools.partial(place_kernel, quarters, len(groups[0])),
        out_shape=jax.ShapeDtypeStruct((count, 4 * wide), f32),
        in_specs=[pl.BlockSpec(memory_space=pltpu.SMEM)] + [hbm] * len(held) + [vmem] * len(sources),
        out_specs=hbm,
        scratch_shapes=[
            pltpu.VMEM((len(quarters), count, wide), f32),
            pltpu.SemaphoreType.DMA((len(quarters),)),
        ],
        input_output_aliases={1: 0} if held else {},
        compiler_params=pltpu.CompilerParams(vmem_limit_bytes=10 << 20),
        name="place",
    )(where, *held, *sources)


def swap(array, axis, bit):
    return lax.ppermute(array, axis, [(i, i ^ bit) for i in range(lax.axis_size(axis))])


def shift(array, axis, steps):
    size = lax.axis_size(axis)
    return lax.ppermute(array, axis, [(i, (i + 2 * steps) % size) for i in range(size)])


def body(
    vectors,
    wear_freq,
    param_scale,
    row_angle,
    row_weight,
    entry_block,
    entry_row,
    entry_count,
    block_home,
):
    holders = lax.axis_size("rows")
    members = lax.axis_size("grp")
    vector_count = vectors.shape[0]
    blocks_here = vectors.shape[1] // BLK_P
    slots = entry_block.shape[0]
    capacity = slots // holders
    width = row_angle.shape[0]

    names = jnp.arange(block_home.shape[0], dtype=jnp.int32)
    stored = jnp.sum(
        jnp.where(entry_block[:, None] == names[None, :], block_home[None, :], 0), axis=1
    )
    slot_ids = jnp.arange(slots, dtype=jnp.int32)
    live = slot_ids < entry_count[0]
    holder = jnp.where(live, stored // blocks_here, -1)
    earlier = (holder[:, None] == holder[None, :]) & (slot_ids[None, :] < slot_ids[:, None])
    places = jnp.sum(earlier.astype(jnp.int32), axis=1)
    code = stored % blocks_here * (width // BLK_R) + entry_row
    target = jnp.where(live, holder * capacity + places, -1)
    room_ids = jnp.arange(holders * capacity, dtype=jnp.int32)
    wanted = (
        jnp.sum(jnp.where(target[None, :] == room_ids[:, None], code[None, :] + 1, 0), axis=1) - 1
    )
    wanted = wanted.reshape(holders, 1, capacity).astype(f32)

    angle_rows = jnp.stack(
        angle_pieces(row_angle.astype(f32)) + [row_weight.astype(f32)], axis=0
    )
    send = jnp.concatenate(
        [
            jnp.broadcast_to(angle_rows[None], (holders, PIECES - 1, width)),
            jnp.pad(wanted, ((0, 0), (0, 0), (0, width - capacity))),
        ],
        axis=1,
    ).astype(bf16)
    left = lax.all_to_all(send, "rows", split_axis=0, concat_axis=0, tiled=True)
    codes = left[:, PIECES - 1, :capacity].astype(jnp.int32).reshape(holders * capacity)

    freq = wear_freq.reshape(blocks_here, 1, BLK_P)
    scale = (param_scale.astype(f32) * (1.0 / math.sqrt(8.0 * BLK_P))).astype(bf16)
    scale = scale.reshape(blocks_here, 1, BLK_P)
    kind = lax.broadcasted_iota(jnp.int32, (1, PIECES, 1), 1)
    right = jnp.concatenate(
        [
            jnp.where(kind < PIECES - 2, freq, jnp.zeros_like(freq)),
            jnp.where(kind == PIECES - 2, scale, jnp.zeros_like(scale)),
        ],
        axis=2,
    )
    me = lax.axis_index("rows")
    core = lax.axis_index("grp") % 2
    side, position = me % 2, me // 2
    ring = holders // 2

    jac = None
    waiting = []
    arrived = []
    for k in range(ring):
        where = jnp.stack([(position + 2 * ring - 1 - k) % ring, side])
        near, far, jac = forward(codes, where, left, right, vectors, capacity, jac)
        waiting.append((near, swap(far, "rows", 1)))
        if k > 0:
            before, got = waiting[k - 1]
            pair = before + got
            if k == ring - 1:
                pair = pair.astype(bf16)
            older = arrived[: ring - 3]
            codes, pair, older = lax.optimization_barrier((codes, pair, older))
            arrived = older + arrived[ring - 3 :]
            arrived.append(shift(pair, "rows", -k))
    near, got = waiting[-1]
    got, early = lax.optimization_barrier((got, arrived[:-1]))
    arrived = early + arrived[-1:]
    outputs = near + got
    for pair in arrived:
        outputs = outputs + pair.astype(f32)
    outputs = outputs.astype(bf16)

    same = [outputs] + [shift(outputs, "rows", k) for k in range(1, ring)]
    pieces = same + [swap(piece, "rows", 1) for piece in same]

    def terms(first, pieces):
        where = jnp.stack([position, side, first])
        return backward(codes, where, jac, pieces, quarter, capacity)

    quarter = blocks_here // 4
    pairs = []
    sums = []
    for chunk in range(2):
        given, pieces = terms((2 * (1 - core) + chunk) * quarter, pieces)
        given = swap(given, "grp", 1)
        kept, pieces = terms((2 * core + chunk) * quarter, pieces)
        chunk_sum = kept + given
        bit = 2
        pair = (chunk_sum, jnp.zeros_like(chunk_sum))
        while bit < members:
            rounded = lax.reduce_precision(chunk_sum, 8, 7)
            sent = rounded.astype(bf16)
            codes, sent, sums = lax.optimization_barrier((codes, sent, sums))
            pair = (sent, swap(sent, "grp", bit))
            chunk_sum = rounded + pair[1].astype(f32)
            bit *= 2
        sums.append(chunk_sum)
        pairs.append(pair)
    where = core.reshape(1)
    early = place(where, None, ((True, 0), (False, 0)), ((sums[0],), (swap(sums[0], "grp", 1),)))
    last = pairs[1]
    across = tuple(swap(array, "grp", 1) for array in last)
    return place(where, early, ((True, 1), (False, 1)), (last, across))


def solution(mesh):
    return jax.shard_map(
        body,
        mesh=mesh,
        in_specs=(
            P(None, "rows"),
            P("rows"),
            P("rows"),
            P(("rows", "grp")),
            P(("rows", "grp")),
            P(("rows", "grp")),
            P(("rows", "grp")),
            P(("rows", "grp")),
            P(),
        ),
        out_specs=P(None, "rows"),
        check_vma=False,
    )
```
